32 devices in a mesh: seq: 4 (over x, core), dp: 4 (over z), tensor: 2 (over y).
Axes of the slice: x: 2, y: 2, z: 4, core: 2. Of those that a mesh axis runs over, the one named last changes fastest.
Arguments:
- queries: bfloat16 [4, 1536, 2048], P('dp', ('seq', 'tensor')), may hold values from -128 to 128
- key_vectors: bfloat16 [4, 1536, 2048], P('dp', ('seq', 'tensor')), may hold values from -6 to 6
- values: bfloat16 [4, 1536, 2048], P('dp', ('seq', 'tensor')), may hold values from -6 to 6
- out_grad: bfloat16 [4, 1536, 2048], P('dp', ('seq', 'tensor')), may hold values from -6 to 6
- positions: int32 [4, 1536], P('dp', 'seq'), may hold values from -1 to 8191, as said below
- sink_logits: float32 [16], P('tensor'), may hold values from -1 to 3
Outputs:
- attended: bfloat16 [4, 1536, 2048], P('dp', ('seq', 'tensor'))
- query_grad: bfloat16 [4, 1536, 2048], P('dp', ('seq', 'tensor'))
- key_grad: bfloat16 [4, 1536, 2048], P('dp', ('seq', 'tensor'))
- value_grad: bfloat16 [4, 1536, 2048], P('dp', ('seq', 'tensor'))
- sink_grad: float32 [16], P('tensor')
The draws below stay inside these ranges and needn't reach their ends.
Inputs may be any that keep to these rules, and one draw needn't show every extreme that they name: Each document's tokens 0 to 8191 form slabs of 4096 tokens; each slab keeps exactly 512 routed tokens, its first half on one sequence shard of 384 slots and its second half on the next. A shard lists its routed positions in rising order in its first slots and -1 in the slots left over; it holds 128 to 384 routed tokens, and some shard of every document holds 384.
All inputs are finite; a program needn't handle non-finite values.
Results may differ from the reference program's by a relative error of at most 0.02.
Values may be sent and summed in bfloat16 or wider, within the bound.
No kernel may reach another device: no remote copies, remote signals or barrier semaphores. Data moves between devices by JAX's collectives and lax.ppermute only.
A program may use at most 128 MiB of HBM per device.

```python
import jax
import jax.numpy as jnp
from jax import lax

SLAB = 4096
HEADS = 16
DH = 128
KEEP = 512
CAP = 384
DOCS = 4
SLOTS = 1536


def query_key_pair(key):
    base_key = jax.random.fold_in(key, 7)
    query_key, key_key = jax.random.split(base_key)
    shape = (DOCS, SLOTS, HEADS * DH)
    query_draw = jnp.clip(jax.random.normal(query_key, shape, jnp.float32), -6.0, 6.0)
    key_draw = jnp.clip(jax.random.normal(key_key, shape, jnp.float32), -6.0, 6.0)
    return (query_draw.astype(jnp.bfloat16), key_draw.astype(jnp.bfloat16))


def draw_queries(key, part):
    return query_key_pair(key)[0]


def draw_key_vectors(key, part):
    return query_key_pair(key)[1]


def draw_positions(key, part):
    base_key = jax.random.fold_in(key, 11)
    count_key, forced_key, choice_key = jax.random.split(base_key, 3)
    half_slab = SLAB // 2
    slab_count = SLOTS // (2 * CAP)
    counts = jax.random.randint(count_key, (DOCS, slab_count), KEEP - CAP, CAP + 1)
    forced = jax.random.randint(forced_key, (DOCS,), 0, slab_count)
    counts = jnp.where(jnp.arange(slab_count)[None, :] == forced[:, None], CAP, counts)
    shard_counts = jnp.stack([counts, KEEP - counts], axis=2).reshape(DOCS * 2 * slab_count)
    shard_keys = jax.random.split(choice_key, DOCS * 2 * slab_count)
    shard_ids = jnp.tile(jnp.arange(2 * slab_count, dtype=jnp.int32), DOCS)

    def one_shard(sub_key, count, shard_id):
        shuffled = jax.random.permutation(sub_key, half_slab)
        ranking = jnp.argsort(shuffled, stable=True)
        chosen = ranking < count
        slot_index = jnp.cumsum(chosen.astype(jnp.int32)) - 1
        slot_index = jnp.where(chosen, slot_index, CAP)
        token_place = jnp.arange(half_slab, dtype=jnp.int32) + shard_id * half_slab
        return jnp.full((CAP,), -1, jnp.int32).at[slot_index].set(token_place, mode='drop')
    lists = jax.vmap(one_shard)(shard_keys, shard_counts, shard_ids)
    return lists.reshape(DOCS, SLOTS)


def shard_levels(own_key, shape, cuts, smallest, largest):
    level, own = 1.0, jax.random.fold_in(own_key, 6)
    for axis_at, blocks in cuts:
        steps = jnp.exp(jax.random.uniform(jax.random.fold_in(own, axis_at), (blocks,), jnp.float32, smallest / len(cuts), largest / len(cuts)))
        level = level * jnp.repeat(steps, shape[axis_at] // blocks).reshape([-1 if axis == axis_at else 1 for axis in range(len(shape))])
    return level


def centred(rng, shape, scale, reach, cuts=(), held_as=jnp.bfloat16):
    entries = jax.random.normal(rng, shape, jnp.float32) * scale
    if len(cuts) > 0:
        entries = shard_levels(rng, shape, cuts, -0.22, 0.18) * entries
    return jnp.clip(entries, min=-reach, max=reach).astype(held_as)


def setup_inputs(seed: int = 0) -> dict:
    splits = jax.random.split(jax.random.key(seed), 7)
    queries = draw_queries(jax.random.fold_in(splits[6], 71), 0)
    key_vectors = draw_key_vectors(jax.random.fold_in(splits[6], 71), 0)
    values = centred(splits[2], (DOCS, SLOTS, HEADS * DH), 1.0, 6.0, ((0, 4), (1, 8)))
    out_grad = centred(splits[3], (DOCS, SLOTS, HEADS * DH), 1.0, 6.0, ((0, 4), (1, 8)))
    positions = draw_positions(jax.random.fold_in(splits[6], 71), 0)
    sink_logits = jnp.clip(-1.0 + 4.0 * jax.random.uniform(splits[5], (HEADS,), jnp.float32) ** shard_levels(splits[5], (HEADS,), ((0, 2),), -0.2, 0.2), -1.0, 3.0)
    return dict(queries=queries, key_vectors=key_vectors, values=values, out_grad=out_grad, positions=positions, sink_logits=sink_logits)


def head_pass(head_inputs, positions_doc):
    query_head, key_head, value_head, grad_head, sink = head_inputs
    raw_scores = jnp.dot(query_head, key_head.T, preferred_element_type=jnp.float32)
    scores = raw_scores * (DH ** -0.5)
    visible = (positions_doc[None, :] <= positions_doc[:, None]) & (positions_doc[None, :] >= 0)
    scores = jnp.where(visible, scores, -1e30)
    row_max = jnp.maximum(jnp.max(scores, axis=1), sink)
    row_total = jnp.exp(sink - row_max) + jnp.sum(jnp.exp(scores - row_max[:, None]), axis=1)
    weights_full = jnp.exp(scores - row_max[:, None]) / row_total[:, None]
    weights_half = weights_full.astype(jnp.bfloat16)
    attended = jnp.dot(weights_half, value_head, preferred_element_type=jnp.float32).astype(jnp.bfloat16)
    delta_rows = jnp.sum(attended.astype(jnp.float32) * grad_head.astype(jnp.float32), axis=1)
    value_dots = jnp.dot(grad_head, value_head.T, preferred_element_type=jnp.float32)
    score_grad = (weights_full * (value_dots - delta_rows[:, None]) * (DH ** -0.5)).astype(jnp.bfloat16)
    query_grad = jnp.dot(score_grad, key_head, preferred_element_type=jnp.float32).astype(jnp.bfloat16)
    key_grad = jnp.dot(score_grad.T, query_head, preferred_element_type=jnp.float32).astype(jnp.bfloat16)
    value_grad = jnp.dot(weights_half.T, grad_head, preferred_element_type=jnp.float32).astype(jnp.bfloat16)
    sink_term = -jnp.sum(jnp.exp(sink - row_max) / row_total * delta_rows)
    return attended, query_grad, key_grad, value_grad, sink_term


def reference(queries, key_vectors, values, out_grad, positions, sink_logits):
    slot_count = queries.shape[1]
    head_count = queries.shape[2] // DH

    def split_heads(matrix):
        return matrix.reshape(slot_count, head_count, DH).transpose(1, 0, 2)

    def join_heads(stacked):
        return stacked.transpose(1, 0, 2).reshape(slot_count, head_count * DH)

    def document_pass(doc_inputs):
        query_doc, key_doc, value_doc, grad_doc, positions_doc = doc_inputs

        def one_head(head_inputs):
            return head_pass(head_inputs, positions_doc)

        outs = lax.map(one_head, (split_heads(query_doc), split_heads(key_doc), split_heads(value_doc), split_heads(grad_doc), sink_logits))
        return join_heads(outs[0]), join_heads(outs[1]), join_heads(outs[2]), join_heads(outs[3]), outs[4]

    attended, query_grad, key_grad, value_grad, sink_terms = lax.map(document_pass, (queries, key_vectors, values, out_grad, positions))
    return attended, query_grad, key_grad, value_grad, jnp.sum(sink_terms, axis=0)
```

```python
import functools

import jax
import jax.numpy as jnp
from jax import lax
from jax.experimental import pallas as pl
from jax.experimental.pallas import tpu as pltpu
from jax.sharding import PartitionSpec as P

DH = 128
SCALE = DH ** (-0.5)
NEG = -1e30
QB = 256
COUNT_ROWS = 16
F32 = jnp.float32
BF16 = jnp.bfloat16
ANY = pl.BlockSpec(memory_space=pl.ANY)
NT = (((1,), (1,)), ((), ()))
NN = (((1,), (0,)), ((), ()))


def dot(a, b, dims):
    return lax.dot_general(a, b, dims, preferred_element_type=F32)


class Plan:
    def __init__(self, seq, tensor, rows, features):
        self.seq, self.tensor, self.rows = seq, tensor, rows
        self.peers = seq * tensor
        self.slots = rows * self.peers
        self.group_heads = features // DH // tensor
        self.heads = self.group_heads // seq

    def where(self):
        return lax.axis_index("seq"), lax.axis_index("tensor")

    def peer(self, k):
        seq_index, tensor_index = self.where()
        return seq_index ^ (k // self.tensor), tensor_index ^ (k % self.tensor)

    def column(self, k, head):
        seq_index, tensor_index = self.peer(k)
        owned = tensor_index * self.group_heads + seq_index * self.heads + head
        return pl.multiple_of(owned * DH, DH)

    def first_row(self, k):
        seq_index, tensor_index = self.peer(k)
        return pl.multiple_of((seq_index * self.tensor + tensor_index) * self.rows, 16)

    def first_count(self, k):
        seq_index, tensor_index = self.peer(k)
        return pl.multiple_of((seq_index * self.tensor + tensor_index) * COUNT_ROWS, 16)


def pack_kernel(plan, head, *refs):
    arrays, count_ref = refs[:4], refs[4]
    outs, sem = refs[5:-1], refs[-1]
    rows = plan.rows
    copies = []
    for k in range(plan.peers):
        for at, array in enumerate(arrays):
            copies.append(
                pltpu.make_async_copy(
                    array.at[0, :, pl.ds(plan.column(k, head), DH)],
                    outs[k].at[pl.ds(at * rows, rows), :],
                    sem,
                )
            )
        copies.append(
            pltpu.make_async_copy(count_ref, outs[k].at[pl.ds(4 * rows, COUNT_ROWS), :], sem)
        )
    for copy in copies:
        copy.start()
    for copy in copies:
        copy.wait()


def pack(plan, head, arrays, count_tile):
    out = jax.ShapeDtypeStruct((4 * plan.rows + COUNT_ROWS, DH), BF16)
    return pl.pallas_call(
        functools.partial(pack_kernel, plan, head),
        out_shape=(out,) * plan.peers,
        in_specs=[ANY] * 5,
        out_specs=(ANY,) * plan.peers,
        scratch_shapes=[pltpu.SemaphoreType.DMA(())],
        name=f"pack{head}",
    )(*arrays, count_tile)


def attention_kernel(plan, head, *refs):
    peers, rows, slots = plan.peers, plan.rows, plan.slots
    sink_ref = refs[0]
    bufs = refs[1 : 1 + peers]
    outs = refs[1 + peers : 1 + 2 * peers]
    sink_out = refs[1 + 2 * peers]
    (x_ref, count_ref, key_slot, query_slot, kt_ref, vt_ref, s_ref, dk_ref, dv_ref, r_ref, sem) = refs[
        2 + 2 * peers :
    ]
    copies = []
    for k in range(peers):
        first = plan.first_row(k)
        for at in range(4):
            copies.append(
                pltpu.make_async_copy(
                    bufs[k].at[pl.ds(at * rows, rows), :],
                    x_ref.at[at, pl.ds(first, rows), :],
                    sem,
                )
            )
        copies.append(
            pltpu.make_async_copy(
                bufs[k].at[pl.ds(4 * rows, COUNT_ROWS), :],
                count_ref.at[pl.ds(plan.first_count(k), COUNT_ROWS), :],
                sem,
            )
        )
    for copy in copies:
        copy.start()
    for copy in copies:
        copy.wait()

    for b in range(peers):
        count = count_ref[b * COUNT_ROWS : b * COUNT_ROWS + 1, :].astype(F32)[:, :1]
        at = lax.broadcasted_iota(jnp.int32, (rows, QB), 0).astype(F32)
        key_slot[b * rows : (b + 1) * rows, :] = jnp.where(at < count, at + b * rows, 1e9)
        at = lax.broadcasted_iota(jnp.int32, (8, slots), 1).astype(F32)
        inside = (at >= b * rows) & (at < b * rows + count)
        if b == 0:
            query_slot[...] = jnp.where(inside, at, -1.0)
        else:
            query_slot[...] = jnp.where(inside, at, query_slot[...])

    own_seq, _ = plan.where()
    local_head = own_seq * plan.heads + head
    sink = sink_ref[local_head]
    kt_ref[...] = x_ref[1].T
    vt_ref[...] = x_ref[2].T
    sink_sum = jnp.zeros((1, QB), F32)
    for j in range(slots // QB):
        here = slice(j * QB, (j + 1) * QB)
        q_j = x_ref[0, here, :]
        g_j = x_ref[3, here, :]
        slot_j = query_slot[0:1, here]
        top = jnp.full((8, QB), sink, F32)
        for b in range(j + 1):
            at = slice(b * QB, (b + 1) * QB)
            s = dot(x_ref[1, at, :], q_j, NT) * SCALE
            s = jnp.where(key_slot[at, :] <= slot_j, s, NEG)
            s_ref[at, :] = s
            top = jnp.maximum(top, jnp.max(s.reshape(QB // 8, 8, QB), axis=0))
        row_max = jnp.max(top, axis=0, keepdims=True)
        total = jnp.zeros((8, QB), F32)
        for b in range(j + 1):
            at = slice(b * QB, (b + 1) * QB)
            e = jnp.exp(s_ref[at, :] - row_max)
            s_ref[at, :] = e
            total = total + jnp.sum(e.reshape(QB // 8, 8, QB), axis=0)
        sink_part = jnp.exp(sink - row_max)
        inverse = 1.0 / (jnp.sum(total, axis=0, keepdims=True) + sink_part)
        attended_t = jnp.zeros((DH, QB), F32)
        for b in range(j + 1):
            at = slice(b * QB, (b + 1) * QB)
            w = s_ref[at, :] * inverse
            s_ref[at, :] = w
            half = w.astype(BF16)
            attended_t = attended_t + dot(vt_ref[:, at], half, NN)
            dv = dot(half, g_j, NN)
            dv_ref[at, :] = dv if b == j else dv_ref[at, :] + dv
        attended_t = attended_t.astype(BF16).astype(F32)
        delta = jnp.sum(attended_t * g_j.astype(F32).T, axis=0, keepdims=True)
        sink_sum = sink_sum - sink_part * inverse * delta
        r_ref[0, here, :] = attended_t.T.astype(BF16)
        query_grad_t = jnp.zeros((DH, QB), F32)
        for b in range(j + 1):
            at = slice(b * QB, (b + 1) * QB)
            dp = dot(x_ref[2, at, :], g_j, NT)
            ds = (s_ref[at, :] * (dp - delta) * SCALE).astype(BF16)
            query_grad_t = query_grad_t + dot(kt_ref[:, at], ds, NN)
            dk = dot(ds, q_j, NN)
            dk_ref[at, :] = dk if b == j else dk_ref[at, :] + dk
        r_ref[1, here, :] = query_grad_t.T.astype(BF16)
    r_ref[2] = dk_ref[...].astype(BF16)
    r_ref[3] = dv_ref[...].astype(BF16)

    copies = []
    for k in range(peers):
        first = plan.first_row(k)
        for at in range(4):
            copies.append(
                pltpu.make_async_copy(
                    r_ref.at[at, pl.ds(first, rows), :],
                    outs[k].at[pl.ds(at * rows, rows), :],
                    sem,
                )
            )
    for copy in copies:
        copy.start()
    total = jnp.sum(sink_sum, axis=1, keepdims=True)
    row = lax.broadcasted_iota(jnp.int32, sink_out.shape, 0)
    sink_out[...] = jnp.where(row == local_head, total, 0.0)
    for copy in copies:
        copy.wait()


def attention(plan, head, sink_logits, bufs):
    out = jax.ShapeDtypeStruct((4 * plan.rows, DH), BF16)
    slots = plan.slots
    sink_rows = -(-plan.group_heads // 8) * 8
    results = pl.pallas_call(
        functools.partial(attention_kernel, plan, head),
        out_shape=(out,) * plan.peers + (jax.ShapeDtypeStruct((sink_rows, DH), F32),),
        in_specs=[pl.BlockSpec(memory_space=pltpu.SMEM)] + [ANY] * plan.peers,
        out_specs=(ANY,) * plan.peers + (pl.BlockSpec(memory_space=pltpu.VMEM),),
        scratch_shapes=[
            pltpu.VMEM((4, slots, DH), BF16),
            pltpu.VMEM((plan.peers * COUNT_ROWS, DH), BF16),
            pltpu.VMEM((slots, QB), F32),
            pltpu.VMEM((8, slots), F32),
            pltpu.VMEM((DH, slots), BF16),
            pltpu.VMEM((DH, slots), BF16),
            pltpu.VMEM((slots, QB), F32),
            pltpu.VMEM((slots, DH), F32),
            pltpu.VMEM((slots, DH), F32),
            pltpu.VMEM((4, slots, DH), BF16),
            pltpu.SemaphoreType.DMA(()),
        ],
        name=f"attention{head}",
    )(sink_logits, *bufs)
    return results[:-1], results[-1]


def unpack_kernel(plan, head, carried, *refs):
    bufs = refs[: plan.peers]
    sem = refs[-1]
    outs = refs[plan.peers + (4 if carried else 0) : -1]
    rows = plan.rows
    copies = []
    for k in range(plan.peers):
        for at, out in enumerate(outs):
            copies.append(
                pltpu.make_async_copy(
                    bufs[k].at[pl.ds(at * rows, rows), :],
                    out.at[0, :, pl.ds(plan.column(k, head), DH)],
                    sem,
                )
            )
    for copy in copies:
        copy.start()
    for copy in copies:
        copy.wait()


def unpack(plan, head, bufs, held, features):
    out = jax.ShapeDtypeStruct((1, plan.rows, features), BF16)
    carried = held is not None
    held = held if carried else ()
    return pl.pallas_call(
        functools.partial(unpack_kernel, plan, head, carried),
        out_shape=(out,) * 4,
        in_specs=[ANY] * (plan.peers + len(held)),
        out_specs=(ANY,) * 4,
        scratch_shapes=[pltpu.SemaphoreType.DMA(())],
        input_output_aliases={plan.peers + at: at for at in range(len(held))},
        name=f"unpack{head}",
    )(*bufs, *held)


def exchange(plan, bufs):
    axes = ("seq", "tensor")
    swapped = [bufs[0]]
    for k in range(1, plan.peers):
        pairs = [(i, i ^ k) for i in range(plan.peers)]
        swapped.append(lax.ppermute(bufs[k], axes, pairs))
    return swapped


def butterfly_sum(value, axis):
    size = lax.axis_size(axis)
    step = 1
    while step < size:
        value = value + lax.ppermute(value, axis, [(i, i ^ step) for i in range(size)])
        step *= 2
    return value


def by_heads(queries, key_vectors, values, out_grad, positions, sink_logits):
    seq, tensor = lax.axis_size("seq"), lax.axis_size("tensor")
    rows, features = queries.shape[1:]
    plan = Plan(seq, tensor, rows, features)
    filled = jnp.sum((positions >= 0).astype(jnp.int32))
    own = jnp.clip(filled - lax.axis_index("tensor") * rows, 0, rows)
    count_tile = jnp.full((COUNT_ROWS, DH), own, BF16)
    arrays = (queries, key_vectors, values, out_grad)
    received = []
    for head in range(plan.heads):
        received.append(exchange(plan, pack(plan, head, arrays, count_tile)))
    outs = None
    sink_sum = None
    for head in range(plan.heads):
        results, sink_part = attention(plan, head, sink_logits, received[head])
        sink_sum = sink_part if sink_sum is None else sink_sum + sink_part
        outs = unpack(plan, head, exchange(plan, results), outs, features)
    for axis in ("seq", "dp"):
        sink_sum = butterfly_sum(sink_sum, axis)
    return (*outs, sink_sum[: plan.group_heads, 0])


def block_scores(query_block, query_pos, key_block, key_pos):
    raw_scores = jnp.einsum(
        "ghd,khd->hgk", query_block, key_block, preferred_element_type=jnp.float32
    )
    scores = raw_scores * DH ** (-0.5)
    visible = (key_pos[None, :] <= query_pos[:, None]) & (key_pos[None, :] >= 0)
    return jnp.where(visible[None], scores, -1e30)


def row_stats(query_rows, query_pos, last_slab, key_all, key_pos, sink_logits, key_span):
    head_count = query_rows.shape[1]
    row_count = query_rows.shape[0]
    start_max = jnp.broadcast_to(sink_logits[:, None], (head_count, row_count))
    start_total = jnp.zeros((head_count, row_count), jnp.float32)

    def row_one_block(block, loop_state):
        row_max, row_total = loop_state
        key_block = lax.dynamic_slice_in_dim(key_all, block * key_span, key_span, 0)
        pos_block = lax.dynamic_slice_in_dim(key_pos, block * key_span, key_span, 0)
        scores = block_scores(query_rows, query_pos, key_block, pos_block)
        new_max = jnp.maximum(row_max, jnp.max(scores, axis=2))
        row_total = row_total * jnp.exp(row_max - new_max) + jnp.sum(
            jnp.exp(scores - new_max[:, :, None]), axis=2
        )
        return (new_max, row_total)

    row_max, row_total = lax.fori_loop(0, last_slab + 1, row_one_block, (start_max, start_total))
    return (row_max, row_total + jnp.exp(sink_logits[:, None] - row_max))


def attend_rows(
    query_rows, query_pos, last_slab, key_all, value_all, key_pos, row_max, row_total, key_span
):

    def attend_one_block(block, summed):
        key_block = lax.dynamic_slice_in_dim(key_all, block * key_span, key_span, 0)
        value_block = lax.dynamic_slice_in_dim(value_all, block * key_span, key_span, 0)
        pos_block = lax.dynamic_slice_in_dim(key_pos, block * key_span, key_span, 0)
        scores = block_scores(query_rows, query_pos, key_block, pos_block)
        weights_half = (jnp.exp(scores - row_max[:, :, None]) / row_total[:, :, None]).astype(
            jnp.bfloat16
        )
        return summed + jnp.einsum(
            "hgk,khd->ghd", weights_half, value_block, preferred_element_type=jnp.float32
        )

    summed = lax.fori_loop(
        0, last_slab + 1, attend_one_block, jnp.zeros(query_rows.shape, jnp.float32)
    )
    return summed.astype(jnp.bfloat16)


def query_grads(
    query_rows,
    grad_rows,
    query_pos,
    last_slab,
    key_all,
    value_all,
    key_pos,
    row_max,
    row_total,
    delta_rows,
    key_span,
    key_sums,
    value_sums,
):

    def query_one_block(block, loop_state):
        query_sum, key_state, value_state = loop_state
        key_block = lax.dynamic_slice_in_dim(key_all, block * key_span, key_span, 0)
        value_block = lax.dynamic_slice_in_dim(value_all, block * key_span, key_span, 0)
        pos_block = lax.dynamic_slice_in_dim(key_pos, block * key_span, key_span, 0)
        scores = block_scores(query_rows, query_pos, key_block, pos_block)
        weights_full = jnp.exp(scores - row_max[:, :, None]) / row_total[:, :, None]
        value_dots = jnp.einsum(
            "ghd,khd->hgk", grad_rows, value_block, preferred_element_type=jnp.float32
        )
        score_grad = (weights_full * (value_dots - delta_rows[:, :, None]) * DH ** (-0.5)).astype(
            jnp.bfloat16
        )
        query_sum = query_sum + jnp.einsum(
            "hgk,khd->ghd", score_grad, key_block, preferred_element_type=jnp.float32
        )
        return (query_sum, key_state, value_state)

    start = (jnp.zeros(query_rows.shape, jnp.float32), key_sums, value_sums)
    query_sum, key_sums, value_sums = lax.fori_loop(0, last_slab + 1, query_one_block, start)
    return (query_sum.astype(jnp.bfloat16), key_sums, value_sums)


def key_grads(
    key_rows,
    value_rows,
    key_pos,
    query_all,
    grad_all,
    query_pos_all,
    max_all,
    total_all,
    delta_all,
    first_slab,
    slab_count,
    query_span,
):

    def key_one_block(block, loop_state):
        key_sum, value_sum = loop_state
        query_block = lax.dynamic_slice_in_dim(query_all, block * query_span, query_span, 0)
        grad_block = lax.dynamic_slice_in_dim(grad_all, block * query_span, query_span, 0)
        pos_block = lax.dynamic_slice_in_dim(query_pos_all, block * query_span, query_span, 0)
        max_block = lax.dynamic_slice_in_dim(max_all, block * query_span, query_span, 1)
        total_block = lax.dynamic_slice_in_dim(total_all, block * query_span, query_span, 1)
        delta_block = lax.dynamic_slice_in_dim(delta_all, block * query_span, query_span, 1)
        scores = block_scores(query_block, pos_block, key_rows, key_pos)
        weights_full = jnp.exp(scores - max_block[:, :, None]) / total_block[:, :, None]
        value_dots = jnp.einsum(
            "ghd,khd->hgk", grad_block, value_rows, preferred_element_type=jnp.float32
        )
        score_grad = (weights_full * (value_dots - delta_block[:, :, None]) * DH ** (-0.5)).astype(
            jnp.bfloat16
        )
        key_sum = key_sum + jnp.einsum(
            "hgk,ghd->khd", score_grad, query_block, preferred_element_type=jnp.float32
        )
        value_sum = value_sum + jnp.einsum(
            "hgk,ghd->khd",
            weights_full.astype(jnp.bfloat16),
            grad_block,
            preferred_element_type=jnp.float32,
        )
        return (key_sum, value_sum)

    zeros = jnp.zeros(key_rows.shape, jnp.float32)
    return lax.fori_loop(first_slab, slab_count, key_one_block, (zeros, zeros))


def by_rows(queries, key_vectors, values, out_grad, positions, sink_logits):
    queries, key_vectors, values, out_grad = (
        lax.all_to_all(queries, "tensor", split_axis=2, concat_axis=1, tiled=True),
        lax.all_to_all(key_vectors, "tensor", split_axis=2, concat_axis=1, tiled=True),
        lax.all_to_all(values, "tensor", split_axis=2, concat_axis=1, tiled=True),
        lax.all_to_all(out_grad, "tensor", split_axis=2, concat_axis=1, tiled=True),
    )
    capacity = queries.shape[1]
    features = queries.shape[2]
    head_count = features // DH
    key_span = 2 * capacity
    seq_count = lax.axis_size("seq")
    seq_index = lax.axis_index("seq")
    query_rows = queries[0].reshape(capacity, head_count, DH)
    key_rows = key_vectors[0].reshape(capacity, head_count, DH)
    value_rows = values[0].reshape(capacity, head_count, DH)
    grad_rows = out_grad[0].reshape(capacity, head_count, DH)
    pos_rows = positions[0]
    key_all, value_all, key_pos = (
        lax.all_gather(key_rows, "seq", axis=0, tiled=True),
        lax.all_gather(value_rows, "seq", axis=0, tiled=True),
        lax.all_gather(pos_rows, "seq", axis=0, tiled=True),
    )
    own_slab = seq_index // 2
    groups = (query_rows, grad_rows, pos_rows, own_slab)
    key_sums = None
    value_sums = None
    sink_sum = jnp.zeros((head_count,), jnp.float32)
    group_rows, group_grads, group_pos, last_slab = groups
    row_max, row_total = row_stats(
        group_rows, group_pos, last_slab, key_all, key_pos, sink_logits, key_span
    )
    attended = attend_rows(
        group_rows, group_pos, last_slab, key_all, value_all, key_pos, row_max, row_total, key_span
    )
    delta_rows = jnp.sum(attended.astype(jnp.float32) * group_grads.astype(jnp.float32), axis=2).T
    sink_sum = sink_sum - jnp.sum(
        jnp.exp(sink_logits[:, None] - row_max) / row_total * delta_rows, axis=1
    )
    query_grad, key_sums, value_sums = query_grads(
        group_rows,
        group_grads,
        group_pos,
        last_slab,
        key_all,
        value_all,
        key_pos,
        row_max,
        row_total,
        delta_rows,
        key_span,
        key_sums,
        value_sums,
    )
    results = (attended, query_grad, row_max, row_total, delta_rows)
    attended = results[0]
    query_grad = results[1]
    own_max = results[2]
    own_total = results[3]
    own_delta = results[4]
    query_all, grad_all, query_pos_all = (
        lax.all_gather(query_rows, "seq", axis=0, tiled=True),
        lax.all_gather(grad_rows, "seq", axis=0, tiled=True),
        lax.all_gather(pos_rows, "seq", axis=0, tiled=True),
    )
    max_all, total_all, delta_all = (
        lax.all_gather(own_max, "seq", axis=1, tiled=True),
        lax.all_gather(own_total, "seq", axis=1, tiled=True),
        lax.all_gather(own_delta, "seq", axis=1, tiled=True),
    )
    key_sum, value_sum = key_grads(
        key_rows,
        value_rows,
        pos_rows,
        query_all,
        grad_all,
        query_pos_all,
        max_all,
        total_all,
        delta_all,
        own_slab,
        seq_count // 2,
        key_span,
    )
    key_grad, value_grad = (
        lax.all_to_all(
            key_sum.astype(jnp.bfloat16).reshape(1, capacity, features),
            "tensor",
            split_axis=1,
            concat_axis=2,
            tiled=True,
        ),
        lax.all_to_all(
            value_sum.astype(jnp.bfloat16).reshape(1, capacity, features),
            "tensor",
            split_axis=1,
            concat_axis=2,
            tiled=True,
        ),
    )
    attended, query_grad = (
        lax.all_to_all(
            attended.reshape(1, capacity, features),
            "tensor",
            split_axis=1,
            concat_axis=2,
            tiled=True,
        ),
        lax.all_to_all(
            query_grad.reshape(1, capacity, features),
            "tensor",
            split_axis=1,
            concat_axis=2,
            tiled=True,
        ),
    )
    sink_grad = lax.psum(sink_sum, ("seq", "dp"))
    return (attended, query_grad, key_grad, value_grad, sink_grad)


def solution(mesh):
    placed = (
        P("dp", ("seq", "tensor"), None),
        P("dp", ("seq", "tensor"), None),
        P("dp", ("seq", "tensor"), None),
        P("dp", ("seq", "tensor"), None),
        P("dp", "seq"),
        P("tensor"),
    )
    sizes = (mesh.shape["seq"], mesh.shape["tensor"], mesh.shape["dp"])

    def on_device(queries, *rest):
        heads = queries.shape[2] // DH
        even = all(size & (size - 1) == 0 for size in sizes)
        aligned = queries.shape[1] % 16 == 0 and queries.shape[1] <= 256
        if even and aligned and heads % (sizes[0] * sizes[1]) == 0:
            return by_heads(queries, *rest)
        return by_rows(queries, *rest)

    return jax.shard_map(
        on_device,
        mesh=mesh,
        in_specs=placed,
        out_specs=(
            P("dp", ("seq", "tensor"), None),
            P("dp", ("seq", "tensor"), None),
            P("dp", ("seq", "tensor"), None),
            P("dp", ("seq", "tensor"), None),
            P("tensor"),
        ),
        check_vma=False,
    )
```

```python
import functools

import jax
import jax.numpy as jnp
from jax import lax
from jax.experimental import pallas as pl
from jax.experimental.pallas import tpu as pltpu
from jax.sharding import PartitionSpec as P

DH = 128
SCALE = DH ** (-0.5)
NEG = -1e30
QB = 256
COUNT_ROWS = 16
F32 = jnp.float32
BF16 = jnp.bfloat16
ANY = pl.BlockSpec(memory_space=pl.ANY)
NT = (((1,), (1,)), ((), ()))
NN = (((1,), (0,)), ((), ()))


def dot(a, b, dims):
    return lax.dot_general(a, b, dims, preferred_element_type=F32)


class Plan:
    def __init__(self, seq, tensor, rows, features):
        self.seq, self.tensor, self.rows = seq, tensor, rows
        self.peers = seq * tensor
        self.slots = rows * self.peers
        self.group_heads = features // DH // tensor
        self.heads = self.group_heads // seq

    def where(self):
        return lax.axis_index("seq"), lax.axis_index("tensor")

    def peer(self, k):
        seq_index, tensor_index = self.where()
        return seq_index ^ (k // self.tensor), tensor_index ^ (k % self.tensor)

    def column(self, k, head):
        seq_index, tensor_index = self.peer(k)
        owned = tensor_index * self.group_heads + seq_index * self.heads + head
        return pl.multiple_of(owned * DH, DH)

    def first_row(self, k):
        seq_index, tensor_index = self.peer(k)
        return pl.multiple_of((seq_index * self.tensor + tensor_index) * self.rows, 16)

    def first_count(self, k):
        seq_index, tensor_index = self.peer(k)
        return pl.multiple_of((seq_index * self.tensor + tensor_index) * COUNT_ROWS, 16)


def pack_kernel(plan, head, *refs):
    arrays, count_ref = refs[:4], refs[4]
    outs, sem = refs[5:-1], refs[-1]
    rows = plan.rows
    copies = []
    for k in range(plan.peers):
        for at, array in enumerate(arrays):
            copies.append(
                pltpu.make_async_copy(
                    array.at[0, :, pl.ds(plan.column(k, head), DH)],
                    outs[k].at[pl.ds(at * rows, rows), :],
                    sem,
                )
            )
        copies.append(
            pltpu.make_async_copy(count_ref, outs[k].at[pl.ds(4 * rows, COUNT_ROWS), :], sem)
        )
    for copy in copies:
        copy.start()
    for copy in copies:
        copy.wait()


def pack(plan, head, arrays, count_tile):
    out = jax.ShapeDtypeStruct((4 * plan.rows + COUNT_ROWS, DH), BF16)
    return pl.pallas_call(
        functools.partial(pack_kernel, plan, head),
        out_shape=(out,) * plan.peers,
        in_specs=[ANY] * 5,
        out_specs=(pl.BlockSpec(memory_space=pltpu.VMEM),) * plan.peers,
        scratch_shapes=[pltpu.SemaphoreType.DMA(())],
        name=f"pack{head}",
    )(*arrays, count_tile)


def attention_kernel(plan, head, *refs):
    peers, rows, slots = plan.peers, plan.rows, plan.slots
    sink_ref = refs[0]
    bufs = refs[1 : 1 + peers]
    outs = refs[1 + peers : 1 + 2 * peers]
    sink_out = refs[1 + 2 * peers]
    (x_ref, count_ref, key_slot, query_slot, kt_ref, vt_ref, s_ref, dk_ref, dv_ref, r_ref, sem) = refs[
        2 + 2 * peers :
    ]
    copies = []
    for k in range(peers):
        first = plan.first_row(k)
        for at in range(4):
            copies.append(
                pltpu.make_async_copy(
                    bufs[k].at[pl.ds(at * rows, rows), :],
                    x_ref.at[at, pl.ds(first, rows), :],
                    sem,
                )
            )
        copies.append(
            pltpu.make_async_copy(
                bufs[k].at[pl.ds(4 * rows, COUNT_ROWS), :],
                count_ref.at[pl.ds(plan.first_count(k), COUNT_ROWS), :],
                sem,
            )
        )
    for copy in copies:
        copy.start()
    for copy in copies:
        copy.wait()

    for b in range(peers):
        count = count_ref[b * COUNT_ROWS : b * COUNT_ROWS + 1, :].astype(F32)[:, :1]
        at = lax.broadcasted_iota(jnp.int32, (rows, QB), 0).astype(F32)
        key_slot[b * rows : (b + 1) * rows, :] = jnp.where(at < count, at + b * rows, 1e9)
        at = lax.broadcasted_iota(jnp.int32, (8, slots), 1).astype(F32)
        inside = (at >= b * rows) & (at < b * rows + count)
        if b == 0:
            query_slot[...] = jnp.where(inside, at, -1.0)
        else:
            query_slot[...] = jnp.where(inside, at, query_slot[...])

    own_seq, _ = plan.where()
    local_head = own_seq * plan.heads + head
    sink = sink_ref[local_head]
    kt_ref[...] = x_ref[1].T
    vt_ref[...] = x_ref[2].T
    sink_sum = jnp.zeros((1, QB), F32)
    for j in range(slots // QB):
        here = slice(j * QB, (j + 1) * QB)
        q_j = x_ref[0, here, :]
        g_j = x_ref[3, here, :]
        slot_j = query_slot[0:1, here]
        top = jnp.full((8, QB), sink, F32)
        for b in range(j + 1):
            at = slice(b * QB, (b + 1) * QB)
            s = dot(x_ref[1, at, :], q_j, NT) * SCALE
            s = jnp.where(key_slot[at, :] <= slot_j, s, NEG)
            s_ref[at, :] = s
            top = jnp.maximum(top, jnp.max(s.reshape(QB // 8, 8, QB), axis=0))
        row_max = jnp.max(top, axis=0, keepdims=True)
        total = jnp.zeros((8, QB), F32)
        for b in range(j + 1):
            at = slice(b * QB, (b + 1) * QB)
            e = jnp.exp(s_ref[at, :] - row_max)
            s_ref[at, :] = e
            total = total + jnp.sum(e.reshape(QB // 8, 8, QB), axis=0)
        sink_part = jnp.exp(sink - row_max)
        inverse = 1.0 / (jnp.sum(total, axis=0, keepdims=True) + sink_part)
        attended_t = jnp.zeros((DH, QB), F32)
        for b in range(j + 1):
            at = slice(b * QB, (b + 1) * QB)
            w = s_ref[at, :] * inverse
            s_ref[at, :] = w
            half = w.astype(BF16)
            attended_t = attended_t + dot(vt_ref[:, at], half, NN)
            dv = dot(half, g_j, NN)
            dv_ref[at, :] = dv if b == j else dv_ref[at, :] + dv
        attended_t = attended_t.astype(BF16).astype(F32)
        delta = jnp.sum(attended_t * g_j.astype(F32).T, axis=0, keepdims=True)
        sink_sum = sink_sum - sink_part * inverse * delta
        r_ref[0, here, :] = attended_t.T.astype(BF16)
        query_grad_t = jnp.zeros((DH, QB), F32)
        for b in range(j + 1):
            at = slice(b * QB, (b + 1) * QB)
            dp = dot(x_ref[2, at, :], g_j, NT)
            ds = (s_ref[at, :] * (dp - delta) * SCALE).astype(BF16)
            query_grad_t = query_grad_t + dot(kt_ref[:, at], ds, NN)
            dk = dot(ds, q_j, NN)
            dk_ref[at, :] = dk if b == j else dk_ref[at, :] + dk
        r_ref[1, here, :] = query_grad_t.T.astype(BF16)
    r_ref[2] = dk_ref[...].astype(BF16)
    r_ref[3] = dv_ref[...].astype(BF16)

    copies = []
    for k in range(peers):
        first = plan.first_row(k)
        for at in range(4):
            copies.append(
                pltpu.make_async_copy(
                    r_ref.at[at, pl.ds(first, rows), :],
                    outs[k].at[pl.ds(at * rows, rows), :],
                    sem,
                )
            )
    for copy in copies:
        copy.start()
    total = jnp.sum(sink_sum, axis=1, keepdims=True)
    row = lax.broadcasted_iota(jnp.int32, sink_out.shape, 0)
    sink_out[...] = jnp.where(row == local_head, total, 0.0)
    for copy in copies:
        copy.wait()


def attention(plan, head, sink_logits, bufs):
    out = jax.ShapeDtypeStruct((4 * plan.rows, DH), BF16)
    slots = plan.slots
    sink_rows = -(-plan.group_heads // 8) * 8
    results = pl.pallas_call(
        functools.partial(attention_kernel, plan, head),
        out_shape=(out,) * plan.peers + (jax.ShapeDtypeStruct((sink_rows, DH), F32),),
        in_specs=[pl.BlockSpec(memory_space=pltpu.SMEM)] + [ANY] * plan.peers,
        out_specs=(ANY,) * plan.peers + (pl.BlockSpec(memory_space=pltpu.VMEM),),
        scratch_shapes=[
            pltpu.VMEM((4, slots, DH), BF16),
            pltpu.VMEM((plan.peers * COUNT_ROWS, DH), BF16),
            pltpu.VMEM((slots, QB), F32),
            pltpu.VMEM((8, slots), F32),
            pltpu.VMEM((DH, slots), BF16),
            pltpu.VMEM((DH, slots), BF16),
            pltpu.VMEM((slots, QB), F32),
            pltpu.VMEM((slots, DH), F32),
            pltpu.VMEM((slots, DH), F32),
            pltpu.VMEM((4, slots, DH), BF16),
            pltpu.SemaphoreType.DMA(()),
        ],
        name=f"attention{head}",
    )(sink_logits, *bufs)
    return results[:-1], results[-1]


def unpack_kernel(plan, head, carried, *refs):
    bufs = refs[: plan.peers]
    sem = refs[-1]
    outs = refs[plan.peers + (4 if carried else 0) : -1]
    rows = plan.rows
    copies = []
    for k in range(plan.peers):
        for at, out in enumerate(outs):
            copies.append(
                pltpu.make_async_copy(
                    bufs[k].at[pl.ds(at * rows, rows), :],
                    out.at[0, :, pl.ds(plan.column(k, head), DH)],
                    sem,
                )
            )
    for copy in copies:
        copy.start()
    for copy in copies:
        copy.wait()


def unpack(plan, head, bufs, held, features):
    out = jax.ShapeDtypeStruct((1, plan.rows, features), BF16)
    carried = held is not None
    held = held if carried else ()
    return pl.pallas_call(
        functools.partial(unpack_kernel, plan, head, carried),
        out_shape=(out,) * 4,
        in_specs=[pl.BlockSpec(memory_space=pltpu.VMEM)] * plan.peers + [ANY] * len(held),
        out_specs=(ANY,) * 4,
        scratch_shapes=[pltpu.SemaphoreType.DMA(())],
        input_output_aliases={plan.peers + at: at for at in range(len(held))},
        name=f"unpack{head}",
    )(*bufs, *held)


def exchange(plan, bufs):
    axes = ("seq", "tensor")
    swapped = [bufs[0]]
    for k in range(1, plan.peers):
        pairs = [(i, i ^ k) for i in range(plan.peers)]
        swapped.append(lax.ppermute(bufs[k], axes, pairs))
    return swapped


def butterfly_sum(value, axis):
    size = lax.axis_size(axis)
    step = 1
    while step < size:
        value = value + lax.ppermute(value, axis, [(i, i ^ step) for i in range(size)])
        step *= 2
    return value


def by_heads(queries, key_vectors, values, out_grad, positions, sink_logits):
    seq, tensor = lax.axis_size("seq"), lax.axis_size("tensor")
    rows, features = queries.shape[1:]
    plan = Plan(seq, tensor, rows, features)
    filled = jnp.sum((positions >= 0).astype(jnp.int32))
    own = jnp.clip(filled - lax.axis_index("tensor") * rows, 0, rows)
    count_tile = jnp.full((COUNT_ROWS, DH), own, BF16)
    arrays = (queries, key_vectors, values, out_grad)
    received = []
    for head in range(plan.heads):
        received.append(exchange(plan, pack(plan, head, arrays, count_tile)))
    outs = None
    sink_sum = None
    for head in range(plan.heads):
        results, sink_part = attention(plan, head, sink_logits, received[head])
        sink_sum = sink_part if sink_sum is None else sink_sum + sink_part
        outs = unpack(plan, head, exchange(plan, results), outs, features)
    for axis in ("seq", "dp"):
        sink_sum = butterfly_sum(sink_sum, axis)
    return (*outs, sink_sum[: plan.group_heads, 0])


def block_scores(query_block, query_pos, key_block, key_pos):
    raw_scores = jnp.einsum(
        "ghd,khd->hgk", query_block, key_block, preferred_element_type=jnp.float32
    )
    scores = raw_scores * DH ** (-0.5)
    visible = (key_pos[None, :] <= query_pos[:, None]) & (key_pos[None, :] >= 0)
    return jnp.where(visible[None], scores, -1e30)


def row_stats(query_rows, query_pos, last_slab, key_all, key_pos, sink_logits, key_span):
    head_count = query_rows.shape[1]
    row_count = query_rows.shape[0]
    start_max = jnp.broadcast_to(sink_logits[:, None], (head_count, row_count))
    start_total = jnp.zeros((head_count, row_count), jnp.float32)

    def row_one_block(block, loop_state):
        row_max, row_total = loop_state
        key_block = lax.dynamic_slice_in_dim(key_all, block * key_span, key_span, 0)
        pos_block = lax.dynamic_slice_in_dim(key_pos, block * key_span, key_span, 0)
        scores = block_scores(query_rows, query_pos, key_block, pos_block)
        new_max = jnp.maximum(row_max, jnp.max(scores, axis=2))
        row_total = row_total * jnp.exp(row_max - new_max) + jnp.sum(
            jnp.exp(scores - new_max[:, :, None]), axis=2
        )
        return (new_max, row_total)

    row_max, row_total = lax.fori_loop(0, last_slab + 1, row_one_block, (start_max, start_total))
    return (row_max, row_total + jnp.exp(sink_logits[:, None] - row_max))


def attend_rows(
    query_rows, query_pos, last_slab, key_all, value_all, key_pos, row_max, row_total, key_span
):

    def attend_one_block(block, summed):
        key_block = lax.dynamic_slice_in_dim(key_all, block * key_span, key_span, 0)
        value_block = lax.dynamic_slice_in_dim(value_all, block * key_span, key_span, 0)
        pos_block = lax.dynamic_slice_in_dim(key_pos, block * key_span, key_span, 0)
        scores = block_scores(query_rows, query_pos, key_block, pos_block)
        weights_half = (jnp.exp(scores - row_max[:, :, None]) / row_total[:, :, None]).astype(
            jnp.bfloat16
        )
        return summed + jnp.einsum(
            "hgk,khd->ghd", weights_half, value_block, preferred_element_type=jnp.float32
        )

    summed = lax.fori_loop(
        0, last_slab + 1, attend_one_block, jnp.zeros(query_rows.shape, jnp.float32)
    )
    return summed.astype(jnp.bfloat16)


def query_grads(
    query_rows,
    grad_rows,
    query_pos,
    last_slab,
    key_all,
    value_all,
    key_pos,
    row_max,
    row_total,
    delta_rows,
    key_span,
    key_sums,
    value_sums,
):

    def query_one_block(block, loop_state):
        query_sum, key_state, value_state = loop_state
        key_block = lax.dynamic_slice_in_dim(key_all, block * key_span, key_span, 0)
        value_block = lax.dynamic_slice_in_dim(value_all, block * key_span, key_span, 0)
        pos_block = lax.dynamic_slice_in_dim(key_pos, block * key_span, key_span, 0)
        scores = block_scores(query_rows, query_pos, key_block, pos_block)
        weights_full = jnp.exp(scores - row_max[:, :, None]) / row_total[:, :, None]
        value_dots = jnp.einsum(
            "ghd,khd->hgk", grad_rows, value_block, preferred_element_type=jnp.float32
        )
        score_grad = (weights_full * (value_dots - delta_rows[:, :, None]) * DH ** (-0.5)).astype(
            jnp.bfloat16
        )
        query_sum = query_sum + jnp.einsum(
            "hgk,khd->ghd", score_grad, key_block, preferred_element_type=jnp.float32
        )
        return (query_sum, key_state, value_state)

    start = (jnp.zeros(query_rows.shape, jnp.float32), key_sums, value_sums)
    query_sum, key_sums, value_sums = lax.fori_loop(0, last_slab + 1, query_one_block, start)
    return (query_sum.astype(jnp.bfloat16), key_sums, value_sums)


def key_grads(
    key_rows,
    value_rows,
    key_pos,
    query_all,
    grad_all,
    query_pos_all,
    max_all,
    total_all,
    delta_all,
    first_slab,
    slab_count,
    query_span,
):

    def key_one_block(block, loop_state):
        key_sum, value_sum = loop_state
        query_block = lax.dynamic_slice_in_dim(query_all, block * query_span, query_span, 0)
        grad_block = lax.dynamic_slice_in_dim(grad_all, block * query_span, query_span, 0)
        pos_block = lax.dynamic_slice_in_dim(query_pos_all, block * query_span, query_span, 0)
        max_block = lax.dynamic_slice_in_dim(max_all, block * query_span, query_span, 1)
        total_block = lax.dynamic_slice_in_dim(total_all, block * query_span, query_span, 1)
        delta_block = lax.dynamic_slice_in_dim(delta_all, block * query_span, query_span, 1)
        scores = block_scores(query_block, pos_block, key_rows, key_pos)
        weights_full = jnp.exp(scores - max_block[:, :, None]) / total_block[:, :, None]
        value_dots = jnp.einsum(
            "ghd,khd->hgk", grad_block, value_rows, preferred_element_type=jnp.float32
        )
        score_grad = (weights_full * (value_dots - delta_block[:, :, None]) * DH ** (-0.5)).astype(
            jnp.bfloat16
        )
        key_sum = key_sum + jnp.einsum(
            "hgk,ghd->khd", score_grad, query_block, preferred_element_type=jnp.float32
        )
        value_sum = value_sum + jnp.einsum(
            "hgk,ghd->khd",
            weights_full.astype(jnp.bfloat16),
            grad_block,
            preferred_element_type=jnp.float32,
        )
        return (key_sum, value_sum)

    zeros = jnp.zeros(key_rows.shape, jnp.float32)
    return lax.fori_loop(first_slab, slab_count, key_one_block, (zeros, zeros))


def by_rows(queries, key_vectors, values, out_grad, positions, sink_logits):
    queries, key_vectors, values, out_grad = (
        lax.all_to_all(queries, "tensor", split_axis=2, concat_axis=1, tiled=True),
        lax.all_to_all(key_vectors, "tensor", split_axis=2, concat_axis=1, tiled=True),
        lax.all_to_all(values, "tensor", split_axis=2, concat_axis=1, tiled=True),
        lax.all_to_all(out_grad, "tensor", split_axis=2, concat_axis=1, tiled=True),
    )
    capacity = queries.shape[1]
    features = queries.shape[2]
    head_count = features // DH
    key_span = 2 * capacity
    seq_count = lax.axis_size("seq")
    seq_index = lax.axis_index("seq")
    query_rows = queries[0].reshape(capacity, head_count, DH)
    key_rows = key_vectors[0].reshape(capacity, head_count, DH)
    value_rows = values[0].reshape(capacity, head_count, DH)
    grad_rows = out_grad[0].reshape(capacity, head_count, DH)
    pos_rows = positions[0]
    key_all, value_all, key_pos = (
        lax.all_gather(key_rows, "seq", axis=0, tiled=True),
        lax.all_gather(value_rows, "seq", axis=0, tiled=True),
        lax.all_gather(pos_rows, "seq", axis=0, tiled=True),
    )
    own_slab = seq_index // 2
    groups = (query_rows, grad_rows, pos_rows, own_slab)
    key_sums = None
    value_sums = None
    sink_sum = jnp.zeros((head_count,), jnp.float32)
    group_rows, group_grads, group_pos, last_slab = groups
    row_max, row_total = row_stats(
        group_rows, group_pos, last_slab, key_all, key_pos, sink_logits, key_span
    )
    attended = attend_rows(
        group_rows, group_pos, last_slab, key_all, value_all, key_pos, row_max, row_total, key_span
    )
    delta_rows = jnp.sum(attended.astype(jnp.float32) * group_grads.astype(jnp.float32), axis=2).T
    sink_sum = sink_sum - jnp.sum(
        jnp.exp(sink_logits[:, None] - row_max) / row_total * delta_rows, axis=1
    )
    query_grad, key_sums, value_sums = query_grads(
        group_rows,
        group_grads,
        group_pos,
        last_slab,
        key_all,
        value_all,
        key_pos,
        row_max,
        row_total,
        delta_rows,
        key_span,
        key_sums,
        value_sums,
    )
    results = (attended, query_grad, row_max, row_total, delta_rows)
    attended = results[0]
    query_grad = results[1]
    own_max = results[2]
    own_total = results[3]
    own_delta = results[4]
    query_all, grad_all, query_pos_all = (
        lax.all_gather(query_rows, "seq", axis=0, tiled=True),
        lax.all_gather(grad_rows, "seq", axis=0, tiled=True),
        lax.all_gather(pos_rows, "seq", axis=0, tiled=True),
    )
    max_all, total_all, delta_all = (
        lax.all_gather(own_max, "seq", axis=1, tiled=True),
        lax.all_gather(own_total, "seq", axis=1, tiled=True),
        lax.all_gather(own_delta, "seq", axis=1, tiled=True),
    )
    key_sum, value_sum = key_grads(
        key_rows,
        value_rows,
        pos_rows,
        query_all,
        grad_all,
        query_pos_all,
        max_all,
        total_all,
        delta_all,
        own_slab,
        seq_count // 2,
        key_span,
    )
    key_grad, value_grad = (
        lax.all_to_all(
            key_sum.astype(jnp.bfloat16).reshape(1, capacity, features),
            "tensor",
            split_axis=1,
            concat_axis=2,
            tiled=True,
        ),
        lax.all_to_all(
            value_sum.astype(jnp.bfloat16).reshape(1, capacity, features),
            "tensor",
            split_axis=1,
            concat_axis=2,
            tiled=True,
        ),
    )
    attended, query_grad = (
        lax.all_to_all(
            attended.reshape(1, capacity, features),
            "tensor",
            split_axis=1,
            concat_axis=2,
            tiled=True,
        ),
        lax.all_to_all(
            query_grad.reshape(1, capacity, features),
            "tensor",
            split_axis=1,
            concat_axis=2,
            tiled=True,
        ),
    )
    sink_grad = lax.psum(sink_sum, ("seq", "dp"))
    return (attended, query_grad, key_grad, value_grad, sink_grad)


def solution(mesh):
    placed = (
        P("dp", ("seq", "tensor"), None),
        P("dp", ("seq", "tensor"), None),
        P("dp", ("seq", "tensor"), None),
        P("dp", ("seq", "tensor"), None),
        P("dp", "seq"),
        P("tensor"),
    )
    sizes = (mesh.shape["seq"], mesh.shape["tensor"], mesh.shape["dp"])

    def on_device(queries, *rest):
        heads = queries.shape[2] // DH
        even = all(size & (size - 1) == 0 for size in sizes)
        aligned = queries.shape[1] % 16 == 0 and queries.shape[1] <= 256
        if even and aligned and heads % (sizes[0] * sizes[1]) == 0:
            return by_heads(queries, *rest)
        return by_rows(queries, *rest)

    return jax.shard_map(
        on_device,
        mesh=mesh,
        in_specs=placed,
        out_specs=(
            P("dp", ("seq", "tensor"), None),
            P("dp", ("seq", "tensor"), None),
            P("dp", ("seq", "tensor"), None),
            P("dp", ("seq", "tensor"), None),
            P("tensor"),
        ),
        check_vma=False,
    )
```

```python
import functools

import jax
import jax.numpy as jnp
from jax import lax
from jax.experimental import pallas as pl
from jax.experimental.pallas import tpu as pltpu
from jax.sharding import PartitionSpec as P

DH = 128
SCALE = DH ** (-0.5)
NEG = -1e30
LOG2E = 1.4426950408889634
KEEP = 512
QB = 256
CUT = 128
COUNT_ROWS = 16
F32 = jnp.float32
BF16 = jnp.bfloat16
ANY = pl.BlockSpec(memory_space=pl.ANY)
IN_VMEM = pl.BlockSpec(memory_space=pltpu.VMEM)
NT = (((1,), (1,)), ((), ()))
NN = (((1,), (0,)), ((), ()))


def dot(a, b, dims):
    return lax.dot_general(a, b, dims, preferred_element_type=F32)


class Plan:
    def __init__(self, seq, tensor, rows, features):
        self.seq, self.tensor, self.rows = seq, tensor, rows
        self.peers = seq * tensor
        self.slots = rows * self.peers
        self.capacity = rows * tensor
        self.slabs = seq // 2
        self.kept = self.slabs * KEEP
        self.group_heads = features // DH // tensor
        self.heads = self.group_heads // seq

    def where(self):
        return lax.axis_index("seq"), lax.axis_index("tensor")

    def peer(self, k):
        seq_index, tensor_index = self.where()
        return seq_index ^ (k // self.tensor), tensor_index ^ (k % self.tensor)

    def column(self, k, head):
        seq_index, tensor_index = self.peer(k)
        owned = tensor_index * self.group_heads + seq_index * self.heads + head
        return pl.multiple_of(owned * DH, DH)

    def first_row(self, k):
        seq_index, tensor_index = self.peer(k)
        return pl.multiple_of((seq_index * self.tensor + tensor_index) * self.rows, 16)

    def first_count(self, k):
        seq_index, tensor_index = self.peer(k)
        return pl.multiple_of((seq_index * self.tensor + tensor_index) * COUNT_ROWS, 16)


def run_copies(copies):
    for copy in copies:
        copy.start()
    for copy in copies:
        copy.wait()


def pack_kernel(plan, head, *refs):
    arrays, positions = refs[:4], refs[4]
    outs, sem = refs[5:-1], refs[-1]
    rows = plan.rows
    copies = []
    for k in range(plan.peers):
        for at, array in enumerate(arrays):
            copies.append(
                pltpu.make_async_copy(
                    array.at[0, :, pl.ds(plan.column(k, head), DH)],
                    outs[k].at[pl.ds(at * rows, rows), :],
                    sem,
                )
            )
    for copy in copies:
        copy.start()
    _, tensor_index = plan.where()
    slot = lax.broadcasted_iota(jnp.int32, positions.shape, 1) - tensor_index * rows
    filled = (positions[...] >= 0) & (slot >= 0) & (slot < rows)
    count = jnp.sum(filled.astype(F32), axis=1, keepdims=True)
    tile = jnp.broadcast_to(count, (COUNT_ROWS, DH)).astype(BF16)
    for k in range(plan.peers):
        outs[k][4 * rows :, :] = tile
    for copy in copies:
        copy.wait()


def pack(plan, head, arrays, positions):
    out = jax.ShapeDtypeStruct((4 * plan.rows + COUNT_ROWS, DH), BF16)
    return pl.pallas_call(
        functools.partial(pack_kernel, plan, head),
        out_shape=(out,) * plan.peers,
        in_specs=[ANY] * 4 + [IN_VMEM],
        out_specs=(IN_VMEM,) * plan.peers,
        scratch_shapes=[pltpu.SemaphoreType.DMA(())],
        name=f"pack{head}",
    )(*arrays, positions)


def selection(rows, columns, shift, limit=None):
    i = lax.broadcasted_iota(jnp.int32, (rows, columns), 0)
    j = lax.broadcasted_iota(jnp.int32, (rows, columns), 1)
    chosen = j == i + shift
    if limit is not None:
        chosen = chosen & (i < limit)
    return jnp.where(chosen, 1.0, 0.0).astype(BF16)


def compact(plan, slab, first_count, x_ref, y_ref):
    capacity = plan.capacity
    base = slab * KEEP
    here = slab * 2 * capacity
    aligned = pl.multiple_of((first_count // 16) * 16, 16)
    rest = first_count - aligned
    head_part = selection(CUT, CUT, -rest)
    cross_part = selection(CUT, 2 * CUT, CUT - rest)
    row = lax.broadcasted_iota(jnp.int32, (CUT, DH), 0)
    for at in range(4):
        y_ref[at, base : base + capacity, :] = x_ref[at, here : here + capacity, :]
        for part in range(capacity // CUT):
            second = here + capacity + part * CUT
            target = pl.ds(pl.multiple_of(base + aligned + part * CUT, 16), CUT)
            if part == 0:
                moved = dot(head_part, x_ref[at, second : second + CUT, :], NN)
                old = y_ref[at, target, :].astype(F32)
                moved = jnp.where(row < rest, old, moved)
            else:
                moved = dot(cross_part, x_ref[at, second - CUT : second + CUT, :], NN)
            y_ref[at, target, :] = moved.astype(BF16)


def spread(plan, slab, first_count, second_count, r_ref, x_ref):
    capacity = plan.capacity
    base = slab * KEEP
    here = slab * 2 * capacity
    aligned = pl.multiple_of((first_count // 16) * 16, 16)
    rest = first_count - aligned
    row = lax.broadcasted_iota(jnp.int32, (capacity, DH), 0)
    for at in range(4):
        kept = r_ref[at, base : base + capacity, :]
        kept = jnp.where(row < first_count, kept.astype(F32), 0.0).astype(BF16)
        x_ref[at, here : here + capacity, :] = kept
    for part in range(capacity // CUT):
        chosen = selection(CUT, 2 * CUT, rest, second_count - part * CUT)
        source = pl.ds(pl.multiple_of(base + aligned + part * CUT, 16), 2 * CUT)
        target = here + capacity + part * CUT
        for at in range(4):
            moved = dot(chosen, r_ref[at, source, :], NN)
            x_ref[at, target : target + CUT, :] = moved.astype(BF16)


def attention_kernel(plan, head, *refs):
    peers, rows = plan.peers, plan.rows
    sink_ref = refs[0]
    bufs = refs[1 : 1 + peers]
    outs = refs[1 + peers : 1 + 2 * peers]
    sink_out = refs[1 + 2 * peers]
    (x_ref, count_ref, y_ref, kt_ref, vt_ref, s_ref, dk_ref, dv_ref, r_ref, sem) = refs[
        2 + 2 * peers :
    ]
    copies = []
    for k in range(peers):
        first = plan.first_row(k)
        for at in range(4):
            copies.append(
                pltpu.make_async_copy(
                    bufs[k].at[pl.ds(at * rows, rows), :],
                    x_ref.at[at, pl.ds(first, rows), :],
                    sem,
                )
            )
        copies.append(
            pltpu.make_async_copy(
                bufs[k].at[pl.ds(4 * rows, COUNT_ROWS), :],
                count_ref.at[pl.ds(plan.first_count(k), COUNT_ROWS), :],
                sem,
            )
        )
    run_copies(copies)

    shard_counts = []
    for shard in range(plan.seq):
        first = shard * plan.tensor * COUNT_ROWS
        tiles = count_ref[first : first + plan.tensor * COUNT_ROWS, :].astype(F32)
        shard_counts.append((jnp.sum(tiles) * (1.0 / (COUNT_ROWS * DH))).astype(jnp.int32))
    for slab in range(plan.slabs):
        compact(plan, slab, shard_counts[2 * slab], x_ref, y_ref)

    own_seq, _ = plan.where()
    local_head = own_seq * plan.heads + head
    sink = sink_ref[local_head]
    kt_ref[...] = y_ref[1, : plan.kept, :].T
    vt_ref[...] = y_ref[2, : plan.kept, :].T
    behind = lax.broadcasted_iota(jnp.int32, (QB, QB), 0) > lax.broadcasted_iota(
        jnp.int32, (QB, QB), 1
    )
    blocks = plan.kept // QB
    sink_sum = jnp.zeros((1, QB), F32)
    state = {}

    def at_block(b):
        return slice(b * QB, (b + 1) * QB)

    def held(j, b):
        return (j % 2, at_block(b))

    def start(j):
        state[j] = dict(
            q=y_ref[0, at_block(j), :],
            g=y_ref[3, at_block(j), :],
            top=None,
            total=None,
            attended=None,
            query_grad=None,
        )

    def add(now, more):
        return more if now is None else now + more

    def scores(j, b):
        own = state[j]
        s = dot(y_ref[1, at_block(b), :], own["q"], NT)
        if b == j:
            s = jnp.where(behind, NEG, s)
        s_ref[held(j, b)] = s
        top = jnp.max(s.reshape(QB // 8, 8, QB), axis=0)
        own["top"] = top if own["top"] is None else jnp.maximum(own["top"], top)

    def row_max(j):
        own = state[j]
        top = jnp.max(own["top"], axis=0, keepdims=True) * (SCALE * LOG2E)
        own["max"] = jnp.maximum(top, sink * LOG2E)

    def exponentials(j, b):
        own = state[j]
        e = jnp.exp2(s_ref[held(j, b)] * (SCALE * LOG2E) - own["max"])
        s_ref[held(j, b)] = e
        own["total"] = add(own["total"], jnp.sum(e.reshape(QB // 8, 8, QB), axis=0))

    def row_total(j):
        own = state[j]
        own["sink"] = jnp.exp2(sink * LOG2E - own["max"])
        own["inverse"] = 1.0 / (jnp.sum(own["total"], axis=0, keepdims=True) + own["sink"])

    def weigh(j, b):
        own = state[j]
        w = s_ref[held(j, b)] * own["inverse"]
        s_ref[held(j, b)] = w
        half = w.astype(BF16)
        own["attended"] = add(own["attended"], dot(vt_ref[:, at_block(b)], half, NN))
        dv = dot(half, own["g"], NN)
        dv_ref[at_block(b), :] = dv if b == j else dv_ref[at_block(b), :] + dv

    def deltas(j):
        own = state[j]
        attended = own["attended"].astype(BF16)
        r_ref[0, at_block(j), :] = attended.T
        own["delta"] = jnp.sum(
            attended.astype(F32) * own["g"].astype(F32).T, axis=0, keepdims=True
        )
        return own["sink"] * own["inverse"] * own["delta"]

    def gradients(j, b):
        own = state[j]
        dp = dot(y_ref[2, at_block(b), :], own["g"], NT)
        ds = (s_ref[held(j, b)] * (dp - own["delta"])).astype(BF16)
        own["query_grad"] = add(own["query_grad"], dot(kt_ref[:, at_block(b)], ds, NN))
        dk = dot(ds, own["q"], NN)
        dk_ref[at_block(b), :] = dk if b == j else dk_ref[at_block(b), :] + dk

    def finish(j):
        r_ref[1, at_block(j), :] = (state[j]["query_grad"] * SCALE).astype(BF16).T

    for j in range(blocks + 1):
        if j < blocks:
            start(j)
            for b in range(j + 1):
                scores(j, b)
            row_max(j)
        for b in range(j + 1):
            if j < blocks:
                exponentials(j, b)
            if b < j:
                gradients(j - 1, b)
        if j > 0:
            finish(j - 1)
        if j < blocks:
            row_total(j)
            for b in range(j + 1):
                weigh(j, b)
            sink_sum = sink_sum - deltas(j)
    r_ref[2, : plan.kept, :] = (dk_ref[...] * SCALE).astype(BF16)
    r_ref[3, : plan.kept, :] = dv_ref[...].astype(BF16)
    for at in range(4):
        r_ref[at, plan.kept :, :] = jnp.zeros((r_ref.shape[1] - plan.kept, DH), BF16)
    for slab in range(plan.slabs):
        spread(plan, slab, shard_counts[2 * slab], shard_counts[2 * slab + 1], r_ref, x_ref)

    copies = []
    for k in range(peers):
        first = plan.first_row(k)
        for at in range(4):
            copies.append(
                pltpu.make_async_copy(
                    x_ref.at[at, pl.ds(first, rows), :],
                    outs[k].at[pl.ds(at * rows, rows), :],
                    sem,
                )
            )
    for copy in copies:
        copy.start()
    total = jnp.sum(sink_sum, axis=1, keepdims=True)
    row = lax.broadcasted_iota(jnp.int32, sink_out.shape, 0)
    sink_out[...] = jnp.where(row == local_head, total, 0.0)
    for copy in copies:
        copy.wait()


def attention(plan, head, sink_logits, bufs):
    out = jax.ShapeDtypeStruct((4 * plan.rows, DH), BF16)
    kept = plan.kept
    reach = kept - KEEP + 2 * plan.capacity + CUT
    sink_rows = -(-plan.group_heads // 8) * 8
    results = pl.pallas_call(
        functools.partial(attention_kernel, plan, head),
        out_shape=(out,) * plan.peers + (jax.ShapeDtypeStruct((sink_rows, DH), F32),),
        in_specs=[pl.BlockSpec(memory_space=pltpu.SMEM)] + [IN_VMEM] * plan.peers,
        out_specs=(IN_VMEM,) * (plan.peers + 1),
        scratch_shapes=[
            pltpu.VMEM((4, plan.slots, DH), BF16),
            pltpu.VMEM((plan.peers * COUNT_ROWS, DH), BF16),
            pltpu.VMEM((4, reach, DH), BF16),
            pltpu.VMEM((DH, kept), BF16),
            pltpu.VMEM((DH, kept), BF16),
            pltpu.VMEM((2, kept, QB), F32),
            pltpu.VMEM((kept, DH), F32),
            pltpu.VMEM((kept, DH), F32),
            pltpu.VMEM((4, reach, DH), BF16),
            pltpu.SemaphoreType.DMA(()),
        ],
        name=f"attention{head}",
    )(sink_logits, *bufs)
    return results[:-1], results[-1]


def unpack_kernel(plan, head, carried, *refs):
    bufs = refs[: plan.peers]
    sem = refs[-1]
    outs = refs[plan.peers + (4 if carried else 0) : -1]
    rows = plan.rows
    copies = []
    for k in range(plan.peers):
        for at, out in enumerate(outs):
            copies.append(
                pltpu.make_async_copy(
                    bufs[k].at[pl.ds(at * rows, rows), :],
                    out.at[0, :, pl.ds(plan.column(k, head), DH)],
                    sem,
                )
            )
    run_copies(copies)


def unpack(plan, head, bufs, held, features):
    out = jax.ShapeDtypeStruct((1, plan.rows, features), BF16)
    carried = held is not None
    held = held if carried else ()
    return pl.pallas_call(
        functools.partial(unpack_kernel, plan, head, carried),
        out_shape=(out,) * 4,
        in_specs=[IN_VMEM] * plan.peers + [ANY] * len(held),
        out_specs=(ANY,) * 4,
        scratch_shapes=[pltpu.SemaphoreType.DMA(())],
        input_output_aliases={plan.peers + at: at for at in range(len(held))},
        name=f"unpack{head}",
    )(*bufs, *held)


def exchange(plan, bufs):
    axes = ("seq", "tensor")
    swapped = [bufs[0]]
    for k in range(1, plan.peers):
        pairs = [(i, i ^ k) for i in range(plan.peers)]
        swapped.append(lax.ppermute(bufs[k], axes, pairs))
    return swapped


def butterfly_sum(value, axis):
    size = lax.axis_size(axis)
    step = 1
    while step < size:
        value = value + lax.ppermute(value, axis, [(i, i ^ step) for i in range(size)])
        step *= 2
    return value


def by_heads(queries, key_vectors, values, out_grad, positions, sink_logits):
    seq, tensor = lax.axis_size("seq"), lax.axis_size("tensor")
    rows, features = queries.shape[1:]
    plan = Plan(seq, tensor, rows, features)
    arrays = (queries, key_vectors, values, out_grad)
    received = []
    for head in range(plan.heads):
        received.append(exchange(plan, pack(plan, head, arrays, positions)))
    outs = None
    sink_sum = None
    for head in range(plan.heads):
        results, sink_part = attention(plan, head, sink_logits, received[head])
        sink_sum = sink_part if sink_sum is None else sink_sum + sink_part
        outs = unpack(plan, head, exchange(plan, results), outs, features)
    for axis in ("seq", "dp"):
        sink_sum = butterfly_sum(sink_sum, axis)
    return (*outs, sink_sum[: plan.group_heads, 0])


def block_scores(query_block, query_pos, key_block, key_pos):
    raw_scores = jnp.einsum(
        "ghd,khd->hgk", query_block, key_block, preferred_element_type=jnp.float32
    )
    scores = raw_scores * DH ** (-0.5)
    visible = (key_pos[None, :] <= query_pos[:, None]) & (key_pos[None, :] >= 0)
    return jnp.where(visible[None], scores, -1e30)


def row_stats(query_rows, query_pos, last_slab, key_all, key_pos, sink_logits, key_span):
    head_count = query_rows.shape[1]
    row_count = query_rows.shape[0]
    start_max = jnp.broadcast_to(sink_logits[:, None], (head_count, row_count))
    start_total = jnp.zeros((head_count, row_count), jnp.float32)

    def row_one_block(block, loop_state):
        row_max, row_total = loop_state
        key_block = lax.dynamic_slice_in_dim(key_all, block * key_span, key_span, 0)
        pos_block = lax.dynamic_slice_in_dim(key_pos, block * key_span, key_span, 0)
        scores = block_scores(query_rows, query_pos, key_block, pos_block)
        new_max = jnp.maximum(row_max, jnp.max(scores, axis=2))
        row_total = row_total * jnp.exp(row_max - new_max) + jnp.sum(
            jnp.exp(scores - new_max[:, :, None]), axis=2
        )
        return (new_max, row_total)

    row_max, row_total = lax.fori_loop(0, last_slab + 1, row_one_block, (start_max, start_total))
    return (row_max, row_total + jnp.exp(sink_logits[:, None] - row_max))


def attend_rows(
    query_rows, query_pos, last_slab, key_all, value_all, key_pos, row_max, row_total, key_span
):

    def attend_one_block(block, summed):
        key_block = lax.dynamic_slice_in_dim(key_all, block * key_span, key_span, 0)
        value_block = lax.dynamic_slice_in_dim(value_all, block * key_span, key_span, 0)
        pos_block = lax.dynamic_slice_in_dim(key_pos, block * key_span, key_span, 0)
        scores = block_scores(query_rows, query_pos, key_block, pos_block)
        weights_half = (jnp.exp(scores - row_max[:, :, None]) / row_total[:, :, None]).astype(
            jnp.bfloat16
        )
        return summed + jnp.einsum(
            "hgk,khd->ghd", weights_half, value_block, preferred_element_type=jnp.float32
        )

    summed = lax.fori_loop(
        0, last_slab + 1, attend_one_block, jnp.zeros(query_rows.shape, jnp.float32)
    )
    return summed.astype(jnp.bfloat16)


def query_grads(
    query_rows,
    grad_rows,
    query_pos,
    last_slab,
    key_all,
    value_all,
    key_pos,
    row_max,
    row_total,
    delta_rows,
    key_span,
    key_sums,
    value_sums,
):

    def query_one_block(block, loop_state):
        query_sum, key_state, value_state = loop_state
        key_block = lax.dynamic_slice_in_dim(key_all, block * key_span, key_span, 0)
        value_block = lax.dynamic_slice_in_dim(value_all, block * key_span, key_span, 0)
        pos_block = lax.dynamic_slice_in_dim(key_pos, block * key_span, key_span, 0)
        scores = block_scores(query_rows, query_pos, key_block, pos_block)
        weights_full = jnp.exp(scores - row_max[:, :, None]) / row_total[:, :, None]
        value_dots = jnp.einsum(
            "ghd,khd->hgk", grad_rows, value_block, preferred_element_type=jnp.float32
        )
        score_grad = (weights_full * (value_dots - delta_rows[:, :, None]) * DH ** (-0.5)).astype(
            jnp.bfloat16
        )
        query_sum = query_sum + jnp.einsum(
            "hgk,khd->ghd", score_grad, key_block, preferred_element_type=jnp.float32
        )
        return (query_sum, key_state, value_state)

    start = (jnp.zeros(query_rows.shape, jnp.float32), key_sums, value_sums)
    query_sum, key_sums, value_sums = lax.fori_loop(0, last_slab + 1, query_one_block, start)
    return (query_sum.astype(jnp.bfloat16), key_sums, value_sums)


def key_grads(
    key_rows,
    value_rows,
    key_pos,
    query_all,
    grad_all,
    query_pos_all,
    max_all,
    total_all,
    delta_all,
    first_slab,
    slab_count,
    query_span,
):

    def key_one_block(block, loop_state):
        key_sum, value_sum = loop_state
        query_block = lax.dynamic_slice_in_dim(query_all, block * query_span, query_span, 0)
        grad_block = lax.dynamic_slice_in_dim(grad_all, block * query_span, query_span, 0)
        pos_block = lax.dynamic_slice_in_dim(query_pos_all, block * query_span, query_span, 0)
        max_block = lax.dynamic_slice_in_dim(max_all, block * query_span, query_span, 1)
        total_block = lax.dynamic_slice_in_dim(total_all, block * query_span, query_span, 1)
        delta_block = lax.dynamic_slice_in_dim(delta_all, block * query_span, query_span, 1)
        scores = block_scores(query_block, pos_block, key_rows, key_pos)
        weights_full = jnp.exp(scores - max_block[:, :, None]) / total_block[:, :, None]
        value_dots = jnp.einsum(
            "ghd,khd->hgk", grad_block, value_rows, preferred_element_type=jnp.float32
        )
        score_grad = (weights_full * (value_dots - delta_block[:, :, None]) * DH ** (-0.5)).astype(
            jnp.bfloat16
        )
        key_sum = key_sum + jnp.einsum(
            "hgk,ghd->khd", score_grad, query_block, preferred_element_type=jnp.float32
        )
        value_sum = value_sum + jnp.einsum(
            "hgk,ghd->khd",
            weights_full.astype(jnp.bfloat16),
            grad_block,
            preferred_element_type=jnp.float32,
        )
        return (key_sum, value_sum)

    zeros = jnp.zeros(key_rows.shape, jnp.float32)
    return lax.fori_loop(first_slab, slab_count, key_one_block, (zeros, zeros))


def by_rows(queries, key_vectors, values, out_grad, positions, sink_logits):
    queries, key_vectors, values, out_grad = (
        lax.all_to_all(queries, "tensor", split_axis=2, concat_axis=1, tiled=True),
        lax.all_to_all(key_vectors, "tensor", split_axis=2, concat_axis=1, tiled=True),
        lax.all_to_all(values, "tensor", split_axis=2, concat_axis=1, tiled=True),
        lax.all_to_all(out_grad, "tensor", split_axis=2, concat_axis=1, tiled=True),
    )
    capacity = queries.shape[1]
    features = queries.shape[2]
    head_count = features // DH
    key_span = 2 * capacity
    seq_count = lax.axis_size("seq")
    seq_index = lax.axis_index("seq")
    query_rows = queries[0].reshape(capacity, head_count, DH)
    key_rows = key_vectors[0].reshape(capacity, head_count, DH)
    value_rows = values[0].reshape(capacity, head_count, DH)
    grad_rows = out_grad[0].reshape(capacity, head_count, DH)
    pos_rows = positions[0]
    key_all, value_all, key_pos = (
        lax.all_gather(key_rows, "seq", axis=0, tiled=True),
        lax.all_gather(value_rows, "seq", axis=0, tiled=True),
        lax.all_gather(pos_rows, "seq", axis=0, tiled=True),
    )
    own_slab = seq_index // 2
    groups = (query_rows, grad_rows, pos_rows, own_slab)
    key_sums = None
    value_sums = None
    sink_sum = jnp.zeros((head_count,), jnp.float32)
    group_rows, group_grads, group_pos, last_slab = groups
    row_max, row_total = row_stats(
        group_rows, group_pos, last_slab, key_all, key_pos, sink_logits, key_span
    )
    attended = attend_rows(
        group_rows, group_pos, last_slab, key_all, value_all, key_pos, row_max, row_total, key_span
    )
    delta_rows = jnp.sum(attended.astype(jnp.float32) * group_grads.astype(jnp.float32), axis=2).T
    sink_sum = sink_sum - jnp.sum(
        jnp.exp(sink_logits[:, None] - row_max) / row_total * delta_rows, axis=1
    )
    query_grad, key_sums, value_sums = query_grads(
        group_rows,
        group_grads,
        group_pos,
        last_slab,
        key_all,
        value_all,
        key_pos,
        row_max,
        row_total,
        delta_rows,
        key_span,
        key_sums,
        value_sums,
    )
    results = (attended, query_grad, row_max, row_total, delta_rows)
    attended = results[0]
    query_grad = results[1]
    own_max = results[2]
    own_total = results[3]
    own_delta = results[4]
    query_all, grad_all, query_pos_all = (
        lax.all_gather(query_rows, "seq", axis=0, tiled=True),
        lax.all_gather(grad_rows, "seq", axis=0, tiled=True),
        lax.all_gather(pos_rows, "seq", axis=0, tiled=True),
    )
    max_all, total_all, delta_all = (
        lax.all_gather(own_max, "seq", axis=1, tiled=True),
        lax.all_gather(own_total, "seq", axis=1, tiled=True),
        lax.all_gather(own_delta, "seq", axis=1, tiled=True),
    )
    key_sum, value_sum = key_grads(
        key_rows,
        value_rows,
        pos_rows,
        query_all,
        grad_all,
        query_pos_all,
        max_all,
        total_all,
        delta_all,
        own_slab,
        seq_count // 2,
        key_span,
    )
    key_grad, value_grad = (
        lax.all_to_all(
            key_sum.astype(jnp.bfloat16).reshape(1, capacity, features),
            "tensor",
            split_axis=1,
            concat_axis=2,
            tiled=True,
        ),
        lax.all_to_all(
            value_sum.astype(jnp.bfloat16).reshape(1, capacity, features),
            "tensor",
            split_axis=1,
            concat_axis=2,
            tiled=True,
        ),
    )
    attended, query_grad = (
        lax.all_to_all(
            attended.reshape(1, capacity, features),
            "tensor",
            split_axis=1,
            concat_axis=2,
            tiled=True,
        ),
        lax.all_to_all(
            query_grad.reshape(1, capacity, features),
            "tensor",
            split_axis=1,
            concat_axis=2,
            tiled=True,
        ),
    )
    sink_grad = lax.psum(sink_sum, ("seq", "dp"))
    return (attended, query_grad, key_grad, value_grad, sink_grad)


def solution(mesh):
    placed = (
        P("dp", ("seq", "tensor"), None),
        P("dp", ("seq", "tensor"), None),
        P("dp", ("seq", "tensor"), None),
        P("dp", ("seq", "tensor"), None),
        P("dp", "seq"),
        P("tensor"),
    )
    sizes = (mesh.shape["seq"], mesh.shape["tensor"], mesh.shape["dp"])

    def on_device(queries, *rest):
        heads = queries.shape[2] // DH
        even = all(size & (size - 1) == 0 for size in sizes)
        rows = queries.shape[1]
        capacity = rows * sizes[1]
        aligned = rows % 16 == 0 and rows <= 256 and capacity % CUT == 0
        aligned = aligned and sizes[0] > 1 and capacity < KEEP <= 4 * capacity // 3
        if even and aligned and heads % (sizes[0] * sizes[1]) == 0:
            return by_heads(queries, *rest)
        return by_rows(queries, *rest)

    return jax.shard_map(
        on_device,
        mesh=mesh,
        in_specs=placed,
        out_specs=(
            P("dp", ("seq", "tensor"), None),
            P("dp", ("seq", "tensor"), None),
            P("dp", ("seq", "tensor"), None),
            P("dp", ("seq", "tensor"), None),
            P("tensor"),
        ),
        check_vma=False,
    )
```

```python
import functools

import jax
import jax.numpy as jnp
from jax import lax
from jax.experimental import pallas as pl
from jax.experimental.pallas import tpu as pltpu
from jax.sharding import PartitionSpec as P


DH = 128
SCALE = DH ** (-0.5)
NEG = -1e30
LOG2E = 1.4426950408889634
KEEP = 512
QB = 256
CUT = 128
COUNT_ROWS = 16
F32 = jnp.float32
BF16 = jnp.bfloat16
ANY = pl.BlockSpec(memory_space=pl.ANY)
IN_VMEM = pl.BlockSpec(memory_space=pltpu.VMEM)
NT = (((1,), (1,)), ((), ()))
NN = (((1,), (0,)), ((), ()))


def dot(a, b, dims):
    return lax.dot_general(a, b, dims, preferred_element_type=F32)


class Plan:
    def __init__(self, seq, tensor, rows, features):
        self.seq, self.tensor, self.rows = seq, tensor, rows
        self.peers = seq * tensor
        self.slots = rows * self.peers
        self.capacity = rows * tensor
        self.slabs = seq // 2
        self.kept = self.slabs * KEEP
        self.group_heads = features // DH // tensor
        self.heads = self.group_heads // seq

    def where(self):
        return lax.axis_index("seq"), lax.axis_index("tensor")

    def peer(self, k):
        seq_index, tensor_index = self.where()
        return seq_index ^ (k // self.tensor), tensor_index ^ (k % self.tensor)

    def column(self, k, head):
        seq_index, tensor_index = self.peer(k)
        owned = tensor_index * self.group_heads + seq_index * self.heads + head
        return pl.multiple_of(owned * DH, DH)

    def first_row(self, k):
        seq_index, tensor_index = self.peer(k)
        return pl.multiple_of((seq_index * self.tensor + tensor_index) * self.rows, 16)

    def first_count(self, k):
        seq_index, tensor_index = self.peer(k)
        return pl.multiple_of((seq_index * self.tensor + tensor_index) * COUNT_ROWS, 16)


def run_copies(copies):
    for copy in copies:
        copy.start()
    for copy in copies:
        copy.wait()


def pack_kernel(plan, head, *refs):
    arrays, positions = refs[:4], refs[4]
    outs, sem = refs[5:-1], refs[-1]
    rows = plan.rows
    copies = []
    for k in range(plan.peers):
        for at, array in enumerate(arrays):
            copies.append(
                pltpu.make_async_copy(
                    array.at[0, :, pl.ds(plan.column(k, head), DH)],
                    outs[k].at[pl.ds(at * rows, rows), :],
                    sem,
                )
            )
    for copy in copies:
        copy.start()
    _, tensor_index = plan.where()
    slot = lax.broadcasted_iota(jnp.int32, positions.shape, 1) - tensor_index * rows
    filled = (positions[...] >= 0) & (slot >= 0) & (slot < rows)
    count = jnp.sum(filled.astype(F32), axis=1, keepdims=True)
    tile = jnp.broadcast_to(count, (COUNT_ROWS, DH)).astype(BF16)
    for k in range(plan.peers):
        outs[k][4 * rows :, :] = tile
    for copy in copies:
        copy.wait()


def pack(plan, head, arrays, positions):
    out = jax.ShapeDtypeStruct((4 * plan.rows + COUNT_ROWS, DH), BF16)
    return pl.pallas_call(
        functools.partial(pack_kernel, plan, head),
        out_shape=(out,) * plan.peers,
        in_specs=[ANY] * 4 + [IN_VMEM],
        out_specs=(IN_VMEM,) * plan.peers,
        scratch_shapes=[pltpu.SemaphoreType.DMA(())],
    )(*arrays, positions)


def selection(rows, columns, shift, limit=None):
    i = lax.broadcasted_iota(jnp.int32, (rows, columns), 0)
    j = lax.broadcasted_iota(jnp.int32, (rows, columns), 1)
    chosen = j == i + shift
    if limit is not None:
        chosen = chosen & (i < limit)
    return jnp.where(chosen, 1.0, 0.0).astype(BF16)


def compact(plan, slab, first_count, x_ref, y_ref):
    capacity = plan.capacity
    base = slab * KEEP
    here = slab * 2 * capacity
    aligned = pl.multiple_of((first_count // 16) * 16, 16)
    rest = first_count - aligned
    head_part = selection(CUT, CUT, -rest)
    cross_part = selection(CUT, 2 * CUT, CUT - rest)
    row = lax.broadcasted_iota(jnp.int32, (CUT, DH), 0)
    for at in range(4):
        y_ref[at, base : base + capacity, :] = x_ref[at, here : here + capacity, :]
        for part in range(capacity // CUT):
            second = here + capacity + part * CUT
            target = pl.ds(pl.multiple_of(base + aligned + part * CUT, 16), CUT)
            if part == 0:
                moved = dot(head_part, x_ref[at, second : second + CUT, :], NN)
                old = y_ref[at, target, :].astype(F32)
                moved = jnp.where(row < rest, old, moved)
            else:
                moved = dot(cross_part, x_ref[at, second - CUT : second + CUT, :], NN)
            y_ref[at, target, :] = moved.astype(BF16)


def spread(plan, slab, first_count, second_count, r_ref, x_ref):
    capacity = plan.capacity
    base = slab * KEEP
    here = slab * 2 * capacity
    aligned = pl.multiple_of((first_count // 16) * 16, 16)
    rest = first_count - aligned
    row = lax.broadcasted_iota(jnp.int32, (capacity, DH), 0)
    for at in range(4):
        kept = r_ref[at, base : base + capacity, :]
        kept = jnp.where(row < first_count, kept.astype(F32), 0.0).astype(BF16)
        x_ref[at, here : here + capacity, :] = kept
    for part in range(capacity // CUT):
        chosen = selection(CUT, 2 * CUT, rest, second_count - part * CUT)
        source = pl.ds(pl.multiple_of(base + aligned + part * CUT, 16), 2 * CUT)
        target = here + capacity + part * CUT
        for at in range(4):
            moved = dot(chosen, r_ref[at, source, :], NN)
            x_ref[at, target : target + CUT, :] = moved.astype(BF16)


def attention_kernel(plan, head, *refs):
    peers, rows = plan.peers, plan.rows
    sink_ref = refs[0]
    bufs = refs[1 : 1 + peers]
    outs = refs[1 + peers : 1 + 2 * peers]
    sink_out = refs[1 + 2 * peers]
    (x_ref, count_ref, y_ref, kt_ref, vt_ref, s_ref, dk_ref, dv_ref, r_ref, sem) = refs[
        2 + 2 * peers :
    ]
    copies = []
    for k in range(peers):
        first = plan.first_row(k)
        for at in range(4):
            copies.append(
                pltpu.make_async_copy(
                    bufs[k].at[pl.ds(at * rows, rows), :],
                    x_ref.at[at, pl.ds(first, rows), :],
                    sem,
                )
            )
        copies.append(
            pltpu.make_async_copy(
                bufs[k].at[pl.ds(4 * rows, COUNT_ROWS), :],
                count_ref.at[pl.ds(plan.first_count(k), COUNT_ROWS), :],
                sem,
            )
        )
    run_copies(copies)

    shard_counts = []
    for shard in range(plan.seq):
        first = shard * plan.tensor * COUNT_ROWS
        tiles = count_ref[first : first + plan.tensor * COUNT_ROWS, :].astype(F32)
        shard_counts.append((jnp.sum(tiles) * (1.0 / (COUNT_ROWS * DH))).astype(jnp.int32))
    for slab in range(plan.slabs):
        compact(plan, slab, shard_counts[2 * slab], x_ref, y_ref)

    own_seq, _ = plan.where()
    local_head = own_seq * plan.heads + head
    sink = sink_ref[local_head]
    kt_ref[...] = y_ref[1, : plan.kept, :].T
    vt_ref[...] = y_ref[2, : plan.kept, :].T
    behind = lax.broadcasted_iota(jnp.int32, (QB, QB), 0) > lax.broadcasted_iota(
        jnp.int32, (QB, QB), 1
    )
    blocks = plan.kept // QB
    sink_sum = jnp.zeros((1, QB), F32)
    state = {}

    def at_block(b):
        return slice(b * QB, (b + 1) * QB)

    def held(j, b):
        return (j % 2, at_block(b))

    def start(j):
        state[j] = dict(
            q=y_ref[0, at_block(j), :],
            g=y_ref[3, at_block(j), :],
            top=None,
            total=None,
            attended=None,
            query_grad=None,
        )

    def add(now, more):
        return more if now is None else now + more

    def scores(j, b):
        own = state[j]
        s = dot(y_ref[1, at_block(b), :], own["q"], NT)
        if b == j:
            s = jnp.where(behind, NEG, s)
        s_ref[held(j, b)] = s
        top = jnp.max(s.reshape(QB // 8, 8, QB), axis=0)
        own["top"] = top if own["top"] is None else jnp.maximum(own["top"], top)

    def row_max(j):
        own = state[j]
        top = jnp.max(own["top"], axis=0, keepdims=True) * (SCALE * LOG2E)
        own["max"] = jnp.maximum(top, sink * LOG2E)

    def exponentials(j, b):
        own = state[j]
        e = jnp.exp2(s_ref[held(j, b)] * (SCALE * LOG2E) - own["max"])
        s_ref[held(j, b)] = e
        own["total"] = add(own["total"], jnp.sum(e.reshape(QB // 8, 8, QB), axis=0))

    def row_total(j):
        own = state[j]
        own["sink"] = jnp.exp2(sink * LOG2E - own["max"])
        own["inverse"] = 1.0 / (jnp.sum(own["total"], axis=0, keepdims=True) + own["sink"])

    def weigh(j, b):
        own = state[j]
        w = s_ref[held(j, b)] * own["inverse"]
        s_ref[held(j, b)] = w
        half = w.astype(BF16)
        own["attended"] = add(own["attended"], dot(vt_ref[:, at_block(b)], half, NN))
        dv = dot(half, own["g"], NN)
        dv_ref[at_block(b), :] = dv if b == j else dv_ref[at_block(b), :] + dv

    def deltas(j):
        own = state[j]
        attended = own["attended"].astype(BF16)
        r_ref[0, at_block(j), :] = attended.T
        own["delta"] = jnp.sum(
            attended.astype(F32) * own["g"].astype(F32).T, axis=0, keepdims=True
        )
        return own["sink"] * own["inverse"] * own["delta"]

    def gradients(j, b):
        own = state[j]
        dp = dot(y_ref[2, at_block(b), :], own["g"], NT)
        ds = (s_ref[held(j, b)] * (dp - own["delta"])).astype(BF16)
        own["query_grad"] = add(own["query_grad"], dot(kt_ref[:, at_block(b)], ds, NN))
        dk = dot(ds, own["q"], NN)
        dk_ref[at_block(b), :] = dk if b == j else dk_ref[at_block(b), :] + dk

    def finish(j):
        r_ref[1, at_block(j), :] = (state[j]["query_grad"] * SCALE).astype(BF16).T

    for j in range(blocks + 1):
        if j < blocks:
            start(j)
            for b in range(j + 1):
                scores(j, b)
            row_max(j)
        for b in range(j + 1):
            if j < blocks:
                exponentials(j, b)
            if b < j:
                gradients(j - 1, b)
        if j > 0:
            finish(j - 1)
        if j < blocks:
            row_total(j)
            for b in range(j + 1):
                weigh(j, b)
            sink_sum = sink_sum - deltas(j)
    r_ref[2, : plan.kept, :] = (dk_ref[...] * SCALE).astype(BF16)
    r_ref[3, : plan.kept, :] = dv_ref[...].astype(BF16)
    for at in range(4):
        r_ref[at, plan.kept :, :] = jnp.zeros((r_ref.shape[1] - plan.kept, DH), BF16)
    for slab in range(plan.slabs):
        spread(plan, slab, shard_counts[2 * slab], shard_counts[2 * slab + 1], r_ref, x_ref)

    copies = []
    for k in range(peers):
        first = plan.first_row(k)
        for at in range(4):
            copies.append(
                pltpu.make_async_copy(
                    x_ref.at[at, pl.ds(first, rows), :],
                    outs[k].at[pl.ds(at * rows, rows), :],
                    sem,
                )
            )
    for copy in copies:
        copy.start()
    total = jnp.sum(sink_sum, axis=1, keepdims=True)
    row = lax.broadcasted_iota(jnp.int32, sink_out.shape, 0)
    sink_out[...] = jnp.where(row == local_head, total, 0.0)
    for copy in copies:
        copy.wait()


def attention(plan, head, sink_logits, bufs):
    out = jax.ShapeDtypeStruct((4 * plan.rows, DH), BF16)
    kept = plan.kept
    reach = kept - KEEP + 2 * plan.capacity + CUT
    sink_rows = -(-plan.group_heads // 8) * 8
    results = pl.pallas_call(
        functools.partial(attention_kernel, plan, head),
        out_shape=(out,) * plan.peers + (jax.ShapeDtypeStruct((sink_rows, DH), F32),),
        in_specs=[pl.BlockSpec(memory_space=pltpu.SMEM)] + [ANY] * plan.peers,
        out_specs=(ANY,) * plan.peers + (IN_VMEM,),
        scratch_shapes=[
            pltpu.VMEM((4, plan.slots, DH), BF16),
            pltpu.VMEM((plan.peers * COUNT_ROWS, DH), BF16),
            pltpu.VMEM((4, reach, DH), BF16),
            pltpu.VMEM((DH, kept), BF16),
            pltpu.VMEM((DH, kept), BF16),
            pltpu.VMEM((2, kept, QB), F32),
            pltpu.VMEM((kept, DH), F32),
            pltpu.VMEM((kept, DH), F32),
            pltpu.VMEM((4, reach, DH), BF16),
            pltpu.SemaphoreType.DMA(()),
        ],
    )(sink_logits, *bufs)
    return results[:-1], results[-1]


def unpack_kernel(plan, head, carried, *refs):
    bufs = refs[: plan.peers]
    sem = refs[-1]
    outs = refs[plan.peers + (4 if carried else 0) : -1]
    rows = plan.rows
    copies = []
    for k in range(plan.peers):
        for at, out in enumerate(outs):
            copies.append(
                pltpu.make_async_copy(
                    bufs[k].at[pl.ds(at * rows, rows), :],
                    out.at[0, :, pl.ds(plan.column(k, head), DH)],
                    sem,
                )
            )
    run_copies(copies)


def unpack(plan, head, bufs, held, features):
    out = jax.ShapeDtypeStruct((1, plan.rows, features), BF16)
    carried = held is not None
    held = held if carried else ()
    return pl.pallas_call(
        functools.partial(unpack_kernel, plan, head, carried),
        out_shape=(out,) * 4,
        in_specs=[IN_VMEM] * plan.peers + [ANY] * len(held),
        out_specs=(ANY,) * 4,
        scratch_shapes=[pltpu.SemaphoreType.DMA(())],
        input_output_aliases={plan.peers + at: at for at in range(len(held))},
    )(*bufs, *held)


def exchange(plan, bufs):
    axes = ("seq", "tensor")
    swapped = [bufs[0]] * plan.peers
    order = sorted(range(1, plan.peers), key=lambda k: (bin(k).count("1"), -k))
    for k in order:
        pairs = [(i, i ^ k) for i in range(plan.peers)]
        swapped[k] = lax.ppermute(bufs[k], axes, pairs)
    return swapped


def swap_sum(value, axis, step):
    pairs = [(i, i ^ step) for i in range(lax.axis_size(axis))]
    return value + lax.ppermute(value, axis, pairs)


def steps_of(axis):
    size = lax.axis_size(axis)
    return [1 << bit for bit in reversed(range(size.bit_length() - 1))]


def by_heads(queries, key_vectors, values, out_grad, positions, sink_logits):
    seq, tensor = lax.axis_size("seq"), lax.axis_size("tensor")
    rows, features = queries.shape[1:]
    plan = Plan(seq, tensor, rows, features)
    arrays = (queries, key_vectors, values, out_grad)
    received = []
    for head in range(plan.heads):
        received.append(exchange(plan, pack(plan, head, arrays, positions)))
    outs = None
    sink_sum = None
    for head in range(plan.heads):
        last = head == plan.heads - 1
        results, sink_part = attention(plan, head, sink_logits, received[head])
        sink_sum = sink_part if sink_sum is None else sink_sum + sink_part
        if last:
            for axis in ("seq", "dp"):
                for step in steps_of(axis):
                    sink_sum = swap_sum(sink_sum, axis, step)
        results = exchange(plan, results)
        outs = unpack(plan, head, results, outs, features)
    return (*outs, sink_sum[: plan.group_heads, 0])


def block_scores(query_block, query_pos, key_block, key_pos):
    raw_scores = jnp.einsum(
        "ghd,khd->hgk", query_block, key_block, preferred_element_type=jnp.float32
    )
    scores = raw_scores * DH ** (-0.5)
    visible = (key_pos[None, :] <= query_pos[:, None]) & (key_pos[None, :] >= 0)
    return jnp.where(visible[None], scores, -1e30)


def row_stats(query_rows, query_pos, last_slab, key_all, key_pos, sink_logits, key_span):
    head_count = query_rows.shape[1]
    row_count = query_rows.shape[0]
    start_max = jnp.broadcast_to(sink_logits[:, None], (head_count, row_count))
    start_total = jnp.zeros((head_count, row_count), jnp.float32)

    def row_one_block(block, loop_state):
        row_max, row_total = loop_state
        key_block = lax.dynamic_slice_in_dim(key_all, block * key_span, key_span, 0)
        pos_block = lax.dynamic_slice_in_dim(key_pos, block * key_span, key_span, 0)
        scores = block_scores(query_rows, query_pos, key_block, pos_block)
        new_max = jnp.maximum(row_max, jnp.max(scores, axis=2))
        row_total = row_total * jnp.exp(row_max - new_max) + jnp.sum(
            jnp.exp(scores - new_max[:, :, None]), axis=2
        )
        return (new_max, row_total)

    row_max, row_total = lax.fori_loop(0, last_slab + 1, row_one_block, (start_max, start_total))
    return (row_max, row_total + jnp.exp(sink_logits[:, None] - row_max))


def attend_rows(
    query_rows, query_pos, last_slab, key_all, value_all, key_pos, row_max, row_total, key_span
):

    def attend_one_block(block, summed):
        key_block = lax.dynamic_slice_in_dim(key_all, block * key_span, key_span, 0)
        value_block = lax.dynamic_slice_in_dim(value_all, block * key_span, key_span, 0)
        pos_block = lax.dynamic_slice_in_dim(key_pos, block * key_span, key_span, 0)
        scores = block_scores(query_rows, query_pos, key_block, pos_block)
        weights_half = (jnp.exp(scores - row_max[:, :, None]) / row_total[:, :, None]).astype(
            jnp.bfloat16
        )
        return summed + jnp.einsum(
            "hgk,khd->ghd", weights_half, value_block, preferred_element_type=jnp.float32
        )

    summed = lax.fori_loop(
        0, last_slab + 1, attend_one_block, jnp.zeros(query_rows.shape, jnp.float32)
    )
    return summed.astype(jnp.bfloat16)


def query_grads(
    query_rows,
    grad_rows,
    query_pos,
    last_slab,
    key_all,
    value_all,
    key_pos,
    row_max,
    row_total,
    delta_rows,
    key_span,
    key_sums,
    value_sums,
):

    def query_one_block(block, loop_state):
        query_sum, key_state, value_state = loop_state
        key_block = lax.dynamic_slice_in_dim(key_all, block * key_span, key_span, 0)
        value_block = lax.dynamic_slice_in_dim(value_all, block * key_span, key_span, 0)
        pos_block = lax.dynamic_slice_in_dim(key_pos, block * key_span, key_span, 0)
        scores = block_scores(query_rows, query_pos, key_block, pos_block)
        weights_full = jnp.exp(scores - row_max[:, :, None]) / row_total[:, :, None]
        value_dots = jnp.einsum(
            "ghd,khd->hgk", grad_rows, value_block, preferred_element_type=jnp.float32
        )
        score_grad = (weights_full * (value_dots - delta_rows[:, :, None]) * DH ** (-0.5)).astype(
            jnp.bfloat16
        )
        query_sum = query_sum + jnp.einsum(
            "hgk,khd->ghd", score_grad, key_block, preferred_element_type=jnp.float32
        )
        return (query_sum, key_state, value_state)

    start = (jnp.zeros(query_rows.shape, jnp.float32), key_sums, value_sums)
    query_sum, key_sums, value_sums = lax.fori_loop(0, last_slab + 1, query_one_block, start)
    return (query_sum.astype(jnp.bfloat16), key_sums, value_sums)


def key_grads(
    key_rows,
    value_rows,
    key_pos,
    query_all,
    grad_all,
    query_pos_all,
    max_all,
    total_all,
    delta_all,
    first_slab,
    slab_count,
    query_span,
):

    def key_one_block(block, loop_state):
        key_sum, value_sum = loop_state
        query_block = lax.dynamic_slice_in_dim(query_all, block * query_span, query_span, 0)
        grad_block = lax.dynamic_slice_in_dim(grad_all, block * query_span, query_span, 0)
        pos_block = lax.dynamic_slice_in_dim(query_pos_all, block * query_span, query_span, 0)
        max_block = lax.dynamic_slice_in_dim(max_all, block * query_span, query_span, 1)
        total_block = lax.dynamic_slice_in_dim(total_all, block * query_span, query_span, 1)
        delta_block = lax.dynamic_slice_in_dim(delta_all, block * query_span, query_span, 1)
        scores = block_scores(query_block, pos_block, key_rows, key_pos)
        weights_full = jnp.exp(scores - max_block[:, :, None]) / total_block[:, :, None]
        value_dots = jnp.einsum(
            "ghd,khd->hgk", grad_block, value_rows, preferred_element_type=jnp.float32
        )
        score_grad = (weights_full * (value_dots - delta_block[:, :, None]) * DH ** (-0.5)).astype(
            jnp.bfloat16
        )
        key_sum = key_sum + jnp.einsum(
            "hgk,ghd->khd", score_grad, query_block, preferred_element_type=jnp.float32
        )
        value_sum = value_sum + jnp.einsum(
            "hgk,ghd->khd",
            weights_full.astype(jnp.bfloat16),
            grad_block,
            preferred_element_type=jnp.float32,
        )
        return (key_sum, value_sum)

    zeros = jnp.zeros(key_rows.shape, jnp.float32)
    return lax.fori_loop(first_slab, slab_count, key_one_block, (zeros, zeros))


def by_rows(queries, key_vectors, values, out_grad, positions, sink_logits):
    queries, key_vectors, values, out_grad = (
        lax.all_to_all(queries, "tensor", split_axis=2, concat_axis=1, tiled=True),
        lax.all_to_all(key_vectors, "tensor", split_axis=2, concat_axis=1, tiled=True),
        lax.all_to_all(values, "tensor", split_axis=2, concat_axis=1, tiled=True),
        lax.all_to_all(out_grad, "tensor", split_axis=2, concat_axis=1, tiled=True),
    )
    capacity = queries.shape[1]
    features = queries.shape[2]
    head_count = features // DH
    key_span = 2 * capacity
    seq_count = lax.axis_size("seq")
    seq_index = lax.axis_index("seq")
    query_rows = queries[0].reshape(capacity, head_count, DH)
    key_rows = key_vectors[0].reshape(capacity, head_count, DH)
    value_rows = values[0].reshape(capacity, head_count, DH)
    grad_rows = out_grad[0].reshape(capacity, head_count, DH)
    pos_rows = positions[0]
    key_all, value_all, key_pos = (
        lax.all_gather(key_rows, "seq", axis=0, tiled=True),
        lax.all_gather(value_rows, "seq", axis=0, tiled=True),
        lax.all_gather(pos_rows, "seq", axis=0, tiled=True),
    )
    own_slab = seq_index // 2
    groups = (query_rows, grad_rows, pos_rows, own_slab)
    key_sums = None
    value_sums = None
    sink_sum = jnp.zeros((head_count,), jnp.float32)
    group_rows, group_grads, group_pos, last_slab = groups
    row_max, row_total = row_stats(
        group_rows, group_pos, last_slab, key_all, key_pos, sink_logits, key_span
    )
    attended = attend_rows(
        group_rows, group_pos, last_slab, key_all, value_all, key_pos, row_max, row_total, key_span
    )
    delta_rows = jnp.sum(attended.astype(jnp.float32) * group_grads.astype(jnp.float32), axis=2).T
    sink_sum = sink_sum - jnp.sum(
        jnp.exp(sink_logits[:, None] - row_max) / row_total * delta_rows, axis=1
    )
    query_grad, key_sums, value_sums = query_grads(
        group_rows,
        group_grads,
        group_pos,
        last_slab,
        key_all,
        value_all,
        key_pos,
        row_max,
        row_total,
        delta_rows,
        key_span,
        key_sums,
        value_sums,
    )
    results = (attended, query_grad, row_max, row_total, delta_rows)
    attended = results[0]
    query_grad = results[1]
    own_max = results[2]
    own_total = results[3]
    own_delta = results[4]
    query_all, grad_all, query_pos_all = (
        lax.all_gather(query_rows, "seq", axis=0, tiled=True),
        lax.all_gather(grad_rows, "seq", axis=0, tiled=True),
        lax.all_gather(pos_rows, "seq", axis=0, tiled=True),
    )
    max_all, total_all, delta_all = (
        lax.all_gather(own_max, "seq", axis=1, tiled=True),
        lax.all_gather(own_total, "seq", axis=1, tiled=True),
        lax.all_gather(own_delta, "seq", axis=1, tiled=True),
    )
    key_sum, value_sum = key_grads(
        key_rows,
        value_rows,
        pos_rows,
        query_all,
        grad_all,
        query_pos_all,
        max_all,
        total_all,
        delta_all,
        own_slab,
        seq_count // 2,
        key_span,
    )
    key_grad, value_grad = (
        lax.all_to_all(
            key_sum.astype(jnp.bfloat16).reshape(1, capacity, features),
            "tensor",
            split_axis=1,
            concat_axis=2,
            tiled=True,
        ),
        lax.all_to_all(
            value_sum.astype(jnp.bfloat16).reshape(1, capacity, features),
            "tensor",
            split_axis=1,
            concat_axis=2,
            tiled=True,
        ),
    )
    attended, query_grad = (
        lax.all_to_all(
            attended.reshape(1, capacity, features),
            "tensor",
            split_axis=1,
            concat_axis=2,
            tiled=True,
        ),
        lax.all_to_all(
            query_grad.reshape(1, capacity, features),
            "tensor",
            split_axis=1,
            concat_axis=2,
            tiled=True,
        ),
    )
    sink_grad = lax.psum(sink_sum, ("seq", "dp"))
    return (attended, query_grad, key_grad, value_grad, sink_grad)


def solution(mesh):
    placed = (
        P("dp", ("seq", "tensor"), None),
        P("dp", ("seq", "tensor"), None),
        P("dp", ("seq", "tensor"), None),
        P("dp", ("seq", "tensor"), None),
        P("dp", "seq"),
        P("tensor"),
    )
    sizes = (mesh.shape["seq"], mesh.shape["tensor"], mesh.shape["dp"])

    def on_device(queries, *rest):
        heads = queries.shape[2] // DH
        even = all(size & (size - 1) == 0 for size in sizes)
        rows = queries.shape[1]
        capacity = rows * sizes[1]
        aligned = rows % 16 == 0 and rows <= 256 and capacity % CUT == 0
        aligned = aligned and sizes[0] > 1 and capacity < KEEP <= 4 * capacity // 3
        if even and aligned and heads % (sizes[0] * sizes[1]) == 0:
            return by_heads(queries, *rest)
        return by_rows(queries, *rest)

    return jax.shard_map(
        on_device,
        mesh=mesh,
        in_specs=placed,
        out_specs=(
            P("dp", ("seq", "tensor"), None),
            P("dp", ("seq", "tensor"), None),
            P("dp", ("seq", "tensor"), None),
            P("dp", ("seq", "tensor"), None),
            P("tensor"),
        ),
        check_vma=False,
    )
```

```python
import functools

import jax
import jax.numpy as jnp
from jax import lax
from jax.experimental import pallas as pl
from jax.experimental.pallas import tpu as pltpu
from jax.sharding import PartitionSpec as P


DH = 128
SCALE = DH ** (-0.5)
NEG = -1e30
LOG2E = 1.4426950408889634
KEEP = 512
QB = 256
CUT = 128
COUNT_ROWS = 16
F32 = jnp.float32
BF16 = jnp.bfloat16
ANY = pl.BlockSpec(memory_space=pl.ANY)
IN_HBM = pl.BlockSpec(memory_space=pltpu.HBM)
IN_VMEM = pl.BlockSpec(memory_space=pltpu.VMEM)
NT = (((1,), (1,)), ((), ()))
NN = (((1,), (0,)), ((), ()))


def dot(a, b, dims):
    return lax.dot_general(a, b, dims, preferred_element_type=F32)


class Plan:
    def __init__(self, seq, tensor, rows, features):
        self.seq, self.tensor, self.rows = seq, tensor, rows
        self.peers = seq * tensor
        self.slots = rows * self.peers
        self.capacity = rows * tensor
        self.slabs = seq // 2
        self.kept = self.slabs * KEEP
        self.group_heads = features // DH // tensor
        self.heads = self.group_heads // seq

    def where(self):
        return lax.axis_index("seq"), lax.axis_index("tensor")

    def peer(self, k):
        seq_index, tensor_index = self.where()
        return seq_index ^ (k // self.tensor), tensor_index ^ (k % self.tensor)

    def column(self, k, head):
        seq_index, tensor_index = self.peer(k)
        owned = tensor_index * self.group_heads + seq_index * self.heads + head
        return pl.multiple_of(owned * DH, DH)

    def first_row(self, k):
        seq_index, tensor_index = self.peer(k)
        return pl.multiple_of((seq_index * self.tensor + tensor_index) * self.rows, 16)

    def first_count(self, k):
        seq_index, tensor_index = self.peer(k)
        return pl.multiple_of((seq_index * self.tensor + tensor_index) * COUNT_ROWS, 16)


def run_copies(copies):
    for copy in copies:
        copy.start()
    for copy in copies:
        copy.wait()


def pack_kernel(plan, head, *refs):
    arrays, positions_hbm = refs[:4], refs[4]
    outs, positions, sem, positions_sem = refs[5:-3], refs[-3], refs[-2], refs[-1]
    rows = plan.rows
    fetch = pltpu.make_async_copy(positions_hbm, positions, positions_sem)
    fetch.start()
    copies = []
    for k in range(plan.peers):
        for at, array in enumerate(arrays):
            copies.append(
                pltpu.make_async_copy(
                    array.at[0, :, pl.ds(plan.column(k, head), DH)],
                    outs[k].at[pl.ds(at * rows, rows), :],
                    sem,
                )
            )
    for copy in copies:
        copy.start()
    _, tensor_index = plan.where()
    slot = lax.broadcasted_iota(jnp.int32, positions.shape, 1) - tensor_index * rows
    fetch.wait()
    filled = (positions[...] >= 0) & (slot >= 0) & (slot < rows)
    count = jnp.sum(filled.astype(F32), axis=1, keepdims=True)
    tile = jnp.broadcast_to(count, (COUNT_ROWS, DH)).astype(BF16)
    for k in range(plan.peers):
        outs[k][4 * rows :, :] = tile
    for copy in copies:
        copy.wait()


def pack(plan, head, arrays, positions):
    out = jax.ShapeDtypeStruct((4 * plan.rows + COUNT_ROWS, DH), BF16)
    return pl.pallas_call(
        functools.partial(pack_kernel, plan, head),
        out_shape=(out,) * plan.peers,
        in_specs=[IN_HBM] * 5,
        out_specs=(IN_VMEM,) * plan.peers,
        scratch_shapes=[
            pltpu.VMEM(positions.shape, jnp.int32),
            pltpu.SemaphoreType.DMA(()),
            pltpu.SemaphoreType.DMA(()),
        ],
        compiler_params=pltpu.CompilerParams(vmem_limit_bytes=6 << 20),
    )(*(pltpu.with_memory_space_constraint(value, pltpu.HBM) for value in (*arrays, positions)))


def selection(rows, columns, shift, limit=None):
    i = lax.broadcasted_iota(jnp.int32, (rows, columns), 0)
    j = lax.broadcasted_iota(jnp.int32, (rows, columns), 1)
    chosen = j == i + shift
    if limit is not None:
        chosen = chosen & (i < limit)
    return jnp.where(chosen, 1.0, 0.0).astype(BF16)


def compact(plan, slab, first_count, x_ref, y_ref):
    capacity = plan.capacity
    base = slab * KEEP
    here = slab * 2 * capacity
    aligned = pl.multiple_of((first_count // 16) * 16, 16)
    rest = first_count - aligned
    head_part = selection(CUT, CUT, -rest)
    cross_part = selection(CUT, 2 * CUT, CUT - rest)
    row = lax.broadcasted_iota(jnp.int32, (CUT, DH), 0)
    for at in range(4):
        y_ref[at, base : base + capacity, :] = x_ref[at, here : here + capacity, :]
        for part in range(capacity // CUT):
            second = here + capacity + part * CUT
            target = pl.ds(pl.multiple_of(base + aligned + part * CUT, 16), CUT)
            if part == 0:
                moved = dot(head_part, x_ref[at, second : second + CUT, :], NN)
                old = y_ref[at, target, :].astype(F32)
                moved = jnp.where(row < rest, old, moved)
            else:
                moved = dot(cross_part, x_ref[at, second - CUT : second + CUT, :], NN)
            y_ref[at, target, :] = moved.astype(BF16)


def spread(plan, slab, first_count, second_count, r_ref, x_ref):
    capacity = plan.capacity
    base = slab * KEEP
    here = slab * 2 * capacity
    aligned = pl.multiple_of((first_count // 16) * 16, 16)
    rest = first_count - aligned
    row = lax.broadcasted_iota(jnp.int32, (capacity, DH), 0)
    for at in range(4):
        kept = r_ref[at, base : base + capacity, :]
        kept = jnp.where(row < first_count, kept.astype(F32), 0.0).astype(BF16)
        x_ref[at, here : here + capacity, :] = kept
    for part in range(capacity // CUT):
        chosen = selection(CUT, 2 * CUT, rest, second_count - part * CUT)
        source = pl.ds(pl.multiple_of(base + aligned + part * CUT, 16), 2 * CUT)
        target = here + capacity + part * CUT
        for at in range(4):
            moved = dot(chosen, r_ref[at, source, :], NN)
            x_ref[at, target : target + CUT, :] = moved.astype(BF16)


def attention_kernel(plan, head, *refs):
    peers, rows = plan.peers, plan.rows
    sink_ref = refs[0]
    bufs = refs[1 : 1 + peers]
    outs = refs[1 + peers : 1 + 2 * peers]
    sink_out = refs[1 + 2 * peers]
    (x_ref, count_ref, y_ref, kt_ref, vt_ref, s_ref, dk_ref, dv_ref, r_ref) = refs[
        2 + 2 * peers :
    ]
    for k in range(peers):
        first = pl.ds(plan.first_row(k), rows)
        for at in range(4):
            x_ref[at, first, :] = bufs[k][at * rows : (at + 1) * rows, :]
        first = pl.ds(plan.first_count(k), COUNT_ROWS)
        count_ref[first, :] = bufs[k][4 * rows :, :]

    shard_counts = []
    for shard in range(plan.seq):
        first = shard * plan.tensor * COUNT_ROWS
        tiles = count_ref[first : first + plan.tensor * COUNT_ROWS, :].astype(F32)
        shard_counts.append((jnp.sum(tiles) * (1.0 / (COUNT_ROWS * DH))).astype(jnp.int32))
    for slab in range(plan.slabs):
        compact(plan, slab, shard_counts[2 * slab], x_ref, y_ref)

    own_seq, _ = plan.where()
    local_head = own_seq * plan.heads + head
    sink = sink_ref[local_head]
    kt_ref[...] = y_ref[1, : plan.kept, :].T
    vt_ref[...] = y_ref[2, : plan.kept, :].T
    behind = lax.broadcasted_iota(jnp.int32, (QB, QB), 0) > lax.broadcasted_iota(
        jnp.int32, (QB, QB), 1
    )
    blocks = plan.kept // QB
    sink_sum = jnp.zeros((1, QB), F32)
    state = {}

    def at_block(b):
        return slice(b * QB, (b + 1) * QB)

    def held(j, b):
        return (j % 2, at_block(b))

    def start(j):
        state[j] = dict(
            q=y_ref[0, at_block(j), :],
            g=y_ref[3, at_block(j), :],
            top=None,
            total=None,
            attended=None,
            query_grad=None,
        )

    def add(now, more):
        return more if now is None else now + more

    def scores(j, b):
        own = state[j]
        s = dot(y_ref[1, at_block(b), :], own["q"], NT)
        if b == j:
            s = jnp.where(behind, NEG, s)
        s_ref[held(j, b)] = s
        top = jnp.max(s.reshape(QB // 8, 8, QB), axis=0)
        own["top"] = top if own["top"] is None else jnp.maximum(own["top"], top)

    def row_max(j):
        own = state[j]
        top = jnp.max(own["top"], axis=0, keepdims=True) * (SCALE * LOG2E)
        own["max"] = jnp.maximum(top, sink * LOG2E)

    def exponentials(j, b):
        own = state[j]
        e = jnp.exp2(s_ref[held(j, b)] * (SCALE * LOG2E) - own["max"])
        s_ref[held(j, b)] = e
        own["total"] = add(own["total"], jnp.sum(e.reshape(QB // 8, 8, QB), axis=0))

    def row_total(j):
        own = state[j]
        own["sink"] = jnp.exp2(sink * LOG2E - own["max"])
        own["inverse"] = 1.0 / (jnp.sum(own["total"], axis=0, keepdims=True) + own["sink"])

    def weigh(j, b):
        own = state[j]
        w = s_ref[held(j, b)] * own["inverse"]
        s_ref[held(j, b)] = w
        half = w.astype(BF16)
        own["attended"] = add(own["attended"], dot(vt_ref[:, at_block(b)], half, NN))
        dv = dot(half, own["g"], NN)
        dv_ref[at_block(b), :] = dv if b == j else dv_ref[at_block(b), :] + dv

    def deltas(j):
        own = state[j]
        attended = own["attended"].astype(BF16)
        r_ref[0, at_block(j), :] = attended.T
        own["delta"] = jnp.sum(
            attended.astype(F32) * own["g"].astype(F32).T, axis=0, keepdims=True
        )
        return own["sink"] * own["inverse"] * own["delta"]

    def gradients(j, b):
        own = state[j]
        dp = dot(y_ref[2, at_block(b), :], own["g"], NT)
        ds = (s_ref[held(j, b)] * (dp - own["delta"])).astype(BF16)
        own["query_grad"] = add(own["query_grad"], dot(kt_ref[:, at_block(b)], ds, NN))
        dk = dot(ds, own["q"], NN)
        dk_ref[at_block(b), :] = dk if b == j else dk_ref[at_block(b), :] + dk

    def finish(j):
        r_ref[1, at_block(j), :] = (state[j]["query_grad"] * SCALE).astype(BF16).T

    for j in range(blocks + 1):
        if j < blocks:
            start(j)
            for b in range(j + 1):
                scores(j, b)
            row_max(j)
        for b in range(j + 1):
            if j < blocks:
                exponentials(j, b)
            if b < j:
                gradients(j - 1, b)
        if j > 0:
            finish(j - 1)
        if j < blocks:
            row_total(j)
            for b in range(j + 1):
                weigh(j, b)
            sink_sum = sink_sum - deltas(j)
    r_ref[2, : plan.kept, :] = (dk_ref[...] * SCALE).astype(BF16)
    r_ref[3, : plan.kept, :] = dv_ref[...].astype(BF16)
    for at in range(4):
        r_ref[at, plan.kept :, :] = jnp.zeros((r_ref.shape[1] - plan.kept, DH), BF16)
    for slab in range(plan.slabs):
        spread(plan, slab, shard_counts[2 * slab], shard_counts[2 * slab + 1], r_ref, x_ref)

    for k in range(peers):
        first = pl.ds(plan.first_row(k), rows)
        for at in range(4):
            outs[k][at * rows : (at + 1) * rows, :] = x_ref[at, first, :]
    total = jnp.sum(sink_sum, axis=1, keepdims=True)
    row = lax.broadcasted_iota(jnp.int32, sink_out.shape, 0)
    sink_out[...] = jnp.where(row == local_head, total, 0.0)


def attention(plan, head, sink_logits, bufs):
    out = jax.ShapeDtypeStruct((4 * plan.rows, DH), BF16)
    kept = plan.kept
    reach = kept - KEEP + 2 * plan.capacity + CUT
    sink_rows = -(-plan.group_heads // 8) * 8
    results = pl.pallas_call(
        functools.partial(attention_kernel, plan, head),
        out_shape=(out,) * plan.peers + (jax.ShapeDtypeStruct((sink_rows, DH), F32),),
        in_specs=[pl.BlockSpec(memory_space=pltpu.SMEM)] + [IN_VMEM] * plan.peers,
        out_specs=(IN_VMEM,) * (plan.peers + 1),
        scratch_shapes=[
            pltpu.VMEM((4, plan.slots, DH), BF16),
            pltpu.VMEM((plan.peers * COUNT_ROWS, DH), BF16),
            pltpu.VMEM((4, reach, DH), BF16),
            pltpu.VMEM((DH, kept), BF16),
            pltpu.VMEM((DH, kept), BF16),
            pltpu.VMEM((2, kept, QB), F32),
            pltpu.VMEM((kept, DH), F32),
            pltpu.VMEM((kept, DH), F32),
            pltpu.VMEM((4, reach, DH), BF16),
        ],
        compiler_params=pltpu.CompilerParams(vmem_limit_bytes=24 << 20),
    )(sink_logits, *bufs)
    return results[:-1], results[-1]


def unpack_kernel(plan, head, carried, *refs):
    bufs = refs[: plan.peers]
    sem = refs[-1]
    outs = refs[plan.peers + (4 if carried else 0) : -1]
    rows = plan.rows
    copies = []
    for k in range(plan.peers):
        for at, out in enumerate(outs):
            copies.append(
                pltpu.make_async_copy(
                    bufs[k].at[pl.ds(at * rows, rows), :],
                    out.at[0, :, pl.ds(plan.column(k, head), DH)],
                    sem,
                )
            )
    run_copies(copies)


def unpack(plan, head, bufs, held, features):
    out = jax.ShapeDtypeStruct((1, plan.rows, features), BF16)
    carried = held is not None
    held = held if carried else ()
    return pl.pallas_call(
        functools.partial(unpack_kernel, plan, head, carried),
        out_shape=(out,) * 4,
        in_specs=[IN_VMEM] * plan.peers + [ANY] * len(held),
        out_specs=(ANY,) * 4,
        scratch_shapes=[pltpu.SemaphoreType.DMA(())],
        input_output_aliases={plan.peers + at: at for at in range(len(held))},
        compiler_params=pltpu.CompilerParams(vmem_limit_bytes=6 << 20),
    )(*bufs, *held)


def exchange(plan, bufs):
    axes = ("seq", "tensor")
    swapped = [bufs[0]] * plan.peers
    order = sorted(range(1, plan.peers), key=lambda k: (bin(k).count("1"), -k))
    for k in order:
        pairs = [(i, i ^ k) for i in range(plan.peers)]
        swapped[k] = lax.ppermute(bufs[k], axes, pairs)
    return swapped


def swap_sum(value, axis, step):
    pairs = [(i, i ^ step) for i in range(lax.axis_size(axis))]
    return value + lax.ppermute(value, axis, pairs)


def steps_of(axis):
    size = lax.axis_size(axis)
    return [1 << bit for bit in reversed(range(size.bit_length() - 1))]


def by_heads(queries, key_vectors, values, out_grad, positions, sink_logits):
    seq, tensor = lax.axis_size("seq"), lax.axis_size("tensor")
    rows, features = queries.shape[1:]
    plan = Plan(seq, tensor, rows, features)
    arrays = (queries, key_vectors, values, out_grad)
    received = []
    for head in range(plan.heads):
        received.append(exchange(plan, pack(plan, head, arrays, positions)))
    outs = None
    sink_sum = None
    for head in range(plan.heads):
        last = head == plan.heads - 1
        results, sink_part = attention(plan, head, sink_logits, received[head])
        sink_sum = sink_part if sink_sum is None else sink_sum + sink_part
        if last:
            for axis in ("seq", "dp"):
                for step in steps_of(axis):
                    sink_sum = swap_sum(sink_sum, axis, step)
        results = exchange(plan, results)
        outs = unpack(plan, head, results, outs, features)
    return (*outs, sink_sum[: plan.group_heads, 0])


def block_scores(query_block, query_pos, key_block, key_pos):
    raw_scores = jnp.einsum(
        "ghd,khd->hgk", query_block, key_block, preferred_element_type=jnp.float32
    )
    scores = raw_scores * DH ** (-0.5)
    visible = (key_pos[None, :] <= query_pos[:, None]) & (key_pos[None, :] >= 0)
    return jnp.where(visible[None], scores, -1e30)


def row_stats(query_rows, query_pos, last_slab, key_all, key_pos, sink_logits, key_span):
    head_count = query_rows.shape[1]
    row_count = query_rows.shape[0]
    start_max = jnp.broadcast_to(sink_logits[:, None], (head_count, row_count))
    start_total = jnp.zeros((head_count, row_count), jnp.float32)

    def row_one_block(block, loop_state):
        row_max, row_total = loop_state
        key_block = lax.dynamic_slice_in_dim(key_all, block * key_span, key_span, 0)
        pos_block = lax.dynamic_slice_in_dim(key_pos, block * key_span, key_span, 0)
        scores = block_scores(query_rows, query_pos, key_block, pos_block)
        new_max = jnp.maximum(row_max, jnp.max(scores, axis=2))
        row_total = row_total * jnp.exp(row_max - new_max) + jnp.sum(
            jnp.exp(scores - new_max[:, :, None]), axis=2
        )
        return (new_max, row_total)

    row_max, row_total = lax.fori_loop(0, last_slab + 1, row_one_block, (start_max, start_total))
    return (row_max, row_total + jnp.exp(sink_logits[:, None] - row_max))


def attend_rows(
    query_rows, query_pos, last_slab, key_all, value_all, key_pos, row_max, row_total, key_span
):

    def attend_one_block(block, summed):
        key_block = lax.dynamic_slice_in_dim(key_all, block * key_span, key_span, 0)
        value_block = lax.dynamic_slice_in_dim(value_all, block * key_span, key_span, 0)
        pos_block = lax.dynamic_slice_in_dim(key_pos, block * key_span, key_span, 0)
        scores = block_scores(query_rows, query_pos, key_block, pos_block)
        weights_half = (jnp.exp(scores - row_max[:, :, None]) / row_total[:, :, None]).astype(
            jnp.bfloat16
        )
        return summed + jnp.einsum(
            "hgk,khd->ghd", weights_half, value_block, preferred_element_type=jnp.float32
        )

    summed = lax.fori_loop(
        0, last_slab + 1, attend_one_block, jnp.zeros(query_rows.shape, jnp.float32)
    )
    return summed.astype(jnp.bfloat16)


def query_grads(
    query_rows,
    grad_rows,
    query_pos,
    last_slab,
    key_all,
    value_all,
    key_pos,
    row_max,
    row_total,
    delta_rows,
    key_span,
    key_sums,
    value_sums,
):

    def query_one_block(block, loop_state):
        query_sum, key_state, value_state = loop_state
        key_block = lax.dynamic_slice_in_dim(key_all, block * key_span, key_span, 0)
        value_block = lax.dynamic_slice_in_dim(value_all, block * key_span, key_span, 0)
        pos_block = lax.dynamic_slice_in_dim(key_pos, block * key_span, key_span, 0)
        scores = block_scores(query_rows, query_pos, key_block, pos_block)
        weights_full = jnp.exp(scores - row_max[:, :, None]) / row_total[:, :, None]
        value_dots = jnp.einsum(
            "ghd,khd->hgk", grad_rows, value_block, preferred_element_type=jnp.float32
        )
        score_grad = (weights_full * (value_dots - delta_rows[:, :, None]) * DH ** (-0.5)).astype(
            jnp.bfloat16
        )
        query_sum = query_sum + jnp.einsum(
            "hgk,khd->ghd", score_grad, key_block, preferred_element_type=jnp.float32
        )
        return (query_sum, key_state, value_state)

    start = (jnp.zeros(query_rows.shape, jnp.float32), key_sums, value_sums)
    query_sum, key_sums, value_sums = lax.fori_loop(0, last_slab + 1, query_one_block, start)
    return (query_sum.astype(jnp.bfloat16), key_sums, value_sums)


def key_grads(
    key_rows,
    value_rows,
    key_pos,
    query_all,
    grad_all,
    query_pos_all,
    max_all,
    total_all,
    delta_all,
    first_slab,
    slab_count,
    query_span,
):

    def key_one_block(block, loop_state):
        key_sum, value_sum = loop_state
        query_block = lax.dynamic_slice_in_dim(query_all, block * query_span, query_span, 0)
        grad_block = lax.dynamic_slice_in_dim(grad_all, block * query_span, query_span, 0)
        pos_block = lax.dynamic_slice_in_dim(query_pos_all, block * query_span, query_span, 0)
        max_block = lax.dynamic_slice_in_dim(max_all, block * query_span, query_span, 1)
        total_block = lax.dynamic_slice_in_dim(total_all, block * query_span, query_span, 1)
        delta_block = lax.dynamic_slice_in_dim(delta_all, block * query_span, query_span, 1)
        scores = block_scores(query_block, pos_block, key_rows, key_pos)
        weights_full = jnp.exp(scores - max_block[:, :, None]) / total_block[:, :, None]
        value_dots = jnp.einsum(
            "ghd,khd->hgk", grad_block, value_rows, preferred_element_type=jnp.float32
        )
        score_grad = (weights_full * (value_dots - delta_block[:, :, None]) * DH ** (-0.5)).astype(
            jnp.bfloat16
        )
        key_sum = key_sum + jnp.einsum(
            "hgk,ghd->khd", score_grad, query_block, preferred_element_type=jnp.float32
        )
        value_sum = value_sum + jnp.einsum(
            "hgk,ghd->khd",
            weights_full.astype(jnp.bfloat16),
            grad_block,
            preferred_element_type=jnp.float32,
        )
        return (key_sum, value_sum)

    zeros = jnp.zeros(key_rows.shape, jnp.float32)
    return lax.fori_loop(first_slab, slab_count, key_one_block, (zeros, zeros))


def by_rows(queries, key_vectors, values, out_grad, positions, sink_logits):
    queries, key_vectors, values, out_grad = (
        lax.all_to_all(queries, "tensor", split_axis=2, concat_axis=1, tiled=True),
        lax.all_to_all(key_vectors, "tensor", split_axis=2, concat_axis=1, tiled=True),
        lax.all_to_all(values, "tensor", split_axis=2, concat_axis=1, tiled=True),
        lax.all_to_all(out_grad, "tensor", split_axis=2, concat_axis=1, tiled=True),
    )
    capacity = queries.shape[1]
    features = queries.shape[2]
    head_count = features // DH
    key_span = 2 * capacity
    seq_count = lax.axis_size("seq")
    seq_index = lax.axis_index("seq")
    query_rows = queries[0].reshape(capacity, head_count, DH)
    key_rows = key_vectors[0].reshape(capacity, head_count, DH)
    value_rows = values[0].reshape(capacity, head_count, DH)
    grad_rows = out_grad[0].reshape(capacity, head_count, DH)
    pos_rows = positions[0]
    key_all, value_all, key_pos = (
        lax.all_gather(key_rows, "seq", axis=0, tiled=True),
        lax.all_gather(value_rows, "seq", axis=0, tiled=True),
        lax.all_gather(pos_rows, "seq", axis=0, tiled=True),
    )
    own_slab = seq_index // 2
    groups = (query_rows, grad_rows, pos_rows, own_slab)
    key_sums = None
    value_sums = None
    sink_sum = jnp.zeros((head_count,), jnp.float32)
    group_rows, group_grads, group_pos, last_slab = groups
    row_max, row_total = row_stats(
        group_rows, group_pos, last_slab, key_all, key_pos, sink_logits, key_span
    )
    attended = attend_rows(
        group_rows, group_pos, last_slab, key_all, value_all, key_pos, row_max, row_total, key_span
    )
    delta_rows = jnp.sum(attended.astype(jnp.float32) * group_grads.astype(jnp.float32), axis=2).T
    sink_sum = sink_sum - jnp.sum(
        jnp.exp(sink_logits[:, None] - row_max) / row_total * delta_rows, axis=1
    )
    query_grad, key_sums, value_sums = query_grads(
        group_rows,
        group_grads,
        group_pos,
        last_slab,
        key_all,
        value_all,
        key_pos,
        row_max,
        row_total,
        delta_rows,
        key_span,
        key_sums,
        value_sums,
    )
    results = (attended, query_grad, row_max, row_total, delta_rows)
    attended = results[0]
    query_grad = results[1]
    own_max = results[2]
    own_total = results[3]
    own_delta = results[4]
    query_all, grad_all, query_pos_all = (
        lax.all_gather(query_rows, "seq", axis=0, tiled=True),
        lax.all_gather(grad_rows, "seq", axis=0, tiled=True),
        lax.all_gather(pos_rows, "seq", axis=0, tiled=True),
    )
    max_all, total_all, delta_all = (
        lax.all_gather(own_max, "seq", axis=1, tiled=True),
        lax.all_gather(own_total, "seq", axis=1, tiled=True),
        lax.all_gather(own_delta, "seq", axis=1, tiled=True),
    )
    key_sum, value_sum = key_grads(
        key_rows,
        value_rows,
        pos_rows,
        query_all,
        grad_all,
        query_pos_all,
        max_all,
        total_all,
        delta_all,
        own_slab,
        seq_count // 2,
        key_span,
    )
    key_grad, value_grad = (
        lax.all_to_all(
            key_sum.astype(jnp.bfloat16).reshape(1, capacity, features),
            "tensor",
            split_axis=1,
            concat_axis=2,
            tiled=True,
        ),
        lax.all_to_all(
            value_sum.astype(jnp.bfloat16).reshape(1, capacity, features),
            "tensor",
            split_axis=1,
            concat_axis=2,
            tiled=True,
        ),
    )
    attended, query_grad = (
        lax.all_to_all(
            attended.reshape(1, capacity, features),
            "tensor",
            split_axis=1,
            concat_axis=2,
            tiled=True,
        ),
        lax.all_to_all(
            query_grad.reshape(1, capacity, features),
            "tensor",
            split_axis=1,
            concat_axis=2,
            tiled=True,
        ),
    )
    sink_grad = lax.psum(sink_sum, ("seq", "dp"))
    return (attended, query_grad, key_grad, value_grad, sink_grad)


def solution(mesh):
    placed = (
        P("dp", ("seq", "tensor"), None),
        P("dp", ("seq", "tensor"), None),
        P("dp", ("seq", "tensor"), None),
        P("dp", ("seq", "tensor"), None),
        P("dp", "seq"),
        P("tensor"),
    )
    sizes = (mesh.shape["seq"], mesh.shape["tensor"], mesh.shape["dp"])

    def on_device(queries, *rest):
        heads = queries.shape[2] // DH
        even = all(size & (size - 1) == 0 for size in sizes)
        rows = queries.shape[1]
        capacity = rows * sizes[1]
        aligned = rows % 16 == 0 and rows <= 256 and capacity % CUT == 0
        aligned = aligned and sizes[0] > 1 and capacity < KEEP <= 4 * capacity // 3
        if even and aligned and heads % (sizes[0] * sizes[1]) == 0:
            return by_heads(queries, *rest)
        return by_rows(queries, *rest)

    return jax.shard_map(
        on_device,
        mesh=mesh,
        in_specs=placed,
        out_specs=(
            P("dp", ("seq", "tensor"), None),
            P("dp", ("seq", "tensor"), None),
            P("dp", ("seq", "tensor"), None),
            P("dp", ("seq", "tensor"), None),
            P("tensor"),
        ),
        check_vma=False,
    )
```

```python
import functools

import jax
import jax.numpy as jnp
from jax import lax
from jax.experimental import pallas as pl
from jax.experimental.pallas import tpu as pltpu
from jax.sharding import PartitionSpec as P


DH = 128
SCALE = DH ** (-0.5)
NEG = -1e30
LOG2E = 1.4426950408889634
KEEP = 512
QB = 256
CUT = 128
COUNT_ROWS = 16
F32 = jnp.float32
BF16 = jnp.bfloat16
ANY = pl.BlockSpec(memory_space=pl.ANY)
IN_HBM = pl.BlockSpec(memory_space=pltpu.HBM)
IN_VMEM = pl.BlockSpec(memory_space=pltpu.VMEM)
NT = (((1,), (1,)), ((), ()))
NN = (((1,), (0,)), ((), ()))


def dot(a, b, dims):
    return lax.dot_general(a, b, dims, preferred_element_type=F32)


class Plan:
    def __init__(self, seq, tensor, rows, features):
        self.seq, self.tensor, self.rows = seq, tensor, rows
        self.peers = seq * tensor
        self.slots = rows * self.peers
        self.capacity = rows * tensor
        self.slabs = seq // 2
        self.kept = self.slabs * KEEP
        self.group_heads = features // DH // tensor
        self.heads = self.group_heads // seq

    def where(self):
        return lax.axis_index("seq"), lax.axis_index("tensor")

    def peer(self, k):
        seq_index, tensor_index = self.where()
        return seq_index ^ (k // self.tensor), tensor_index ^ (k % self.tensor)

    def column(self, k, head):
        seq_index, tensor_index = self.peer(k)
        owned = tensor_index * self.group_heads + seq_index * self.heads + head
        return pl.multiple_of(owned * DH, DH)

    def first_row(self, k):
        seq_index, tensor_index = self.peer(k)
        return pl.multiple_of((seq_index * self.tensor + tensor_index) * self.rows, 16)

    def first_count(self, k):
        seq_index, tensor_index = self.peer(k)
        return pl.multiple_of((seq_index * self.tensor + tensor_index) * COUNT_ROWS, 16)


def run_copies(copies):
    for copy in copies:
        copy.start()
    for copy in copies:
        copy.wait()


def pack_kernel(plan, head, peers, *refs):
    arrays, positions_hbm = refs[:4], refs[4]
    outs, positions, sem, positions_sem = refs[5:-3], refs[-3], refs[-2], refs[-1]
    rows = plan.rows
    copies = []
    for k, out in zip(peers, outs):
        for at, array in enumerate(arrays):
            copies.append(
                pltpu.make_async_copy(
                    array.at[0, :, pl.ds(plan.column(k, head), DH)],
                    out.at[pl.ds(at * rows, rows), :],
                    sem,
                )
            )
    if head > 0:
        run_copies(copies)
        return
    fetch = pltpu.make_async_copy(positions_hbm, positions, positions_sem)
    fetch.start()
    for copy in copies:
        copy.start()
    _, tensor_index = plan.where()
    slot = lax.broadcasted_iota(jnp.int32, positions.shape, 1) - tensor_index * rows
    fetch.wait()
    filled = (positions[...] >= 0) & (slot >= 0) & (slot < rows)
    count = jnp.sum(filled.astype(F32), axis=1, keepdims=True)
    tile = jnp.broadcast_to(count, (COUNT_ROWS, DH)).astype(BF16)
    for out in outs:
        out[4 * rows :, :] = tile
    for copy in copies:
        copy.wait()


def pack(plan, head, peers, arrays, positions):
    out = jax.ShapeDtypeStruct((4 * plan.rows + (COUNT_ROWS if head == 0 else 0), DH), BF16)
    return pl.pallas_call(
        functools.partial(pack_kernel, plan, head, peers),
        out_shape=(out,) * len(peers),
        in_specs=[IN_HBM] * 5,
        out_specs=(IN_VMEM,) * len(peers),
        scratch_shapes=[
            pltpu.VMEM(positions.shape, jnp.int32),
            pltpu.SemaphoreType.DMA(()),
            pltpu.SemaphoreType.DMA(()),
        ],
        compiler_params=pltpu.CompilerParams(vmem_limit_bytes=6 << 20),
    )(*(pltpu.with_memory_space_constraint(value, pltpu.HBM) for value in (*arrays, positions)))


def selection(rows, columns, shift, limit=None):
    i = lax.broadcasted_iota(jnp.int32, (rows, columns), 0)
    j = lax.broadcasted_iota(jnp.int32, (rows, columns), 1)
    chosen = j == i + shift
    if limit is not None:
        chosen = chosen & (i < limit)
    return jnp.where(chosen, 1.0, 0.0).astype(BF16)


def compact(plan, slab, first_count, x_ref, y_ref):
    capacity = plan.capacity
    base = slab * KEEP
    here = slab * 2 * capacity
    aligned = pl.multiple_of((first_count // 16) * 16, 16)
    rest = first_count - aligned
    head_part = selection(CUT, CUT, -rest)
    cross_part = selection(CUT, 2 * CUT, CUT - rest)
    row = lax.broadcasted_iota(jnp.int32, (CUT, DH), 0)
    for at in range(4):
        y_ref[at, base : base + capacity, :] = x_ref[at, here : here + capacity, :]
        for part in range(capacity // CUT):
            second = here + capacity + part * CUT
            target = pl.ds(pl.multiple_of(base + aligned + part * CUT, 16), CUT)
            if part == 0:
                moved = dot(head_part, x_ref[at, second : second + CUT, :], NN)
                old = y_ref[at, target, :].astype(F32)
                moved = jnp.where(row < rest, old, moved)
            else:
                moved = dot(cross_part, x_ref[at, second - CUT : second + CUT, :], NN)
            y_ref[at, target, :] = moved.astype(BF16)


def spread(plan, slab, first_count, second_count, r_ref, x_ref):
    capacity = plan.capacity
    base = slab * KEEP
    here = slab * 2 * capacity
    aligned = pl.multiple_of((first_count // 16) * 16, 16)
    rest = first_count - aligned
    row = lax.broadcasted_iota(jnp.int32, (capacity, DH), 0)
    for at in range(4):
        kept = r_ref[at, base : base + capacity, :]
        kept = jnp.where(row < first_count, kept.astype(F32), 0.0).astype(BF16)
        x_ref[at, here : here + capacity, :] = kept
    for part in range(capacity // CUT):
        chosen = selection(CUT, 2 * CUT, rest, second_count - part * CUT)
        source = pl.ds(pl.multiple_of(base + aligned + part * CUT, 16), 2 * CUT)
        target = here + capacity + part * CUT
        for at in range(4):
            moved = dot(chosen, r_ref[at, source, :], NN)
            x_ref[at, target : target + CUT, :] = moved.astype(BF16)


def attention_kernel(plan, head, *refs):
    peers, rows = plan.peers, plan.rows
    sink_ref, bufs, refs = refs[0], refs[1 : 1 + peers], refs[1 + peers :]
    if head > 0:
        count_ref, *refs = refs
    outs, sink_out, refs = refs[:peers], refs[peers], refs[peers + 1 :]
    if head == 0:
        count_ref, *refs = refs
        for k in range(peers):
            first = pl.ds(plan.first_count(k), COUNT_ROWS)
            count_ref[first, :] = bufs[k][4 * rows :, :]
    x_ref, y_ref, kt_ref, vt_ref, s_ref, dk_ref, dv_ref, r_ref = refs
    for k in range(peers):
        first = pl.ds(plan.first_row(k), rows)
        for at in range(4):
            x_ref[at, first, :] = bufs[k][at * rows : (at + 1) * rows, :]

    shard_counts = []
    for shard in range(plan.seq):
        first = shard * plan.tensor * COUNT_ROWS
        tiles = count_ref[first : first + plan.tensor * COUNT_ROWS, :].astype(F32)
        shard_counts.append((jnp.sum(tiles) * (1.0 / (COUNT_ROWS * DH))).astype(jnp.int32))
    for slab in range(plan.slabs):
        compact(plan, slab, shard_counts[2 * slab], x_ref, y_ref)

    own_seq, _ = plan.where()
    local_head = own_seq * plan.heads + head
    sink = sink_ref[local_head]
    kt_ref[...] = y_ref[1, : plan.kept, :].T
    vt_ref[...] = y_ref[2, : plan.kept, :].T
    behind = lax.broadcasted_iota(jnp.int32, (QB, QB), 0) > lax.broadcasted_iota(
        jnp.int32, (QB, QB), 1
    )
    blocks = plan.kept // QB
    sink_sum = jnp.zeros((1, QB), F32)
    state = {}

    def at_block(b):
        return slice(b * QB, (b + 1) * QB)

    def held(j, b):
        return (j % 2, at_block(b))

    def start(j):
        state[j] = dict(
            q=y_ref[0, at_block(j), :],
            g=y_ref[3, at_block(j), :],
            top=None,
            total=None,
            attended=None,
            query_grad=None,
        )

    def add(now, more):
        return more if now is None else now + more

    def scores(j, b):
        own = state[j]
        s = dot(y_ref[1, at_block(b), :], own["q"], NT)
        if b == j:
            s = jnp.where(behind, NEG, s)
        s_ref[held(j, b)] = s
        top = jnp.max(s.reshape(QB // 8, 8, QB), axis=0)
        own["top"] = top if own["top"] is None else jnp.maximum(own["top"], top)

    def row_max(j):
        own = state[j]
        top = jnp.max(own["top"], axis=0, keepdims=True) * (SCALE * LOG2E)
        own["max"] = jnp.maximum(top, sink * LOG2E)

    def exponentials(j, b):
        own = state[j]
        e = jnp.exp2(s_ref[held(j, b)] * (SCALE * LOG2E) - own["max"])
        s_ref[held(j, b)] = e
        own["total"] = add(own["total"], jnp.sum(e.reshape(QB // 8, 8, QB), axis=0))

    def row_total(j):
        own = state[j]
        own["sink"] = jnp.exp2(sink * LOG2E - own["max"])
        own["inverse"] = 1.0 / (jnp.sum(own["total"], axis=0, keepdims=True) + own["sink"])

    def weigh(j, b):
        own = state[j]
        w = s_ref[held(j, b)] * own["inverse"]
        s_ref[held(j, b)] = w
        half = w.astype(BF16)
        own["attended"] = add(own["attended"], dot(vt_ref[:, at_block(b)], half, NN))
        dv = dot(half, own["g"], NN)
        dv_ref[at_block(b), :] = dv if b == j else dv_ref[at_block(b), :] + dv

    def deltas(j):
        own = state[j]
        attended = own["attended"].astype(BF16)
        r_ref[0, at_block(j), :] = attended.T
        own["delta"] = jnp.sum(
            attended.astype(F32) * own["g"].astype(F32).T, axis=0, keepdims=True
        )
        return own["sink"] * own["inverse"] * own["delta"]

    def gradients(j, b):
        own = state[j]
        dp = dot(y_ref[2, at_block(b), :], own["g"], NT)
        ds = (s_ref[held(j, b)] * (dp - own["delta"])).astype(BF16)
        own["query_grad"] = add(own["query_grad"], dot(kt_ref[:, at_block(b)], ds, NN))
        dk = dot(ds, own["q"], NN)
        dk_ref[at_block(b), :] = dk if b == j else dk_ref[at_block(b), :] + dk

    def finish(j):
        r_ref[1, at_block(j), :] = (state[j]["query_grad"] * SCALE).astype(BF16).T

    for j in range(blocks + 1):
        if j < blocks:
            start(j)
            for b in range(j + 1):
                scores(j, b)
            row_max(j)
        for b in range(j + 1):
            if j < blocks:
                exponentials(j, b)
            if b < j:
                gradients(j - 1, b)
        if j > 0:
            finish(j - 1)
        if j < blocks:
            row_total(j)
            for b in range(j + 1):
                weigh(j, b)
            sink_sum = sink_sum - deltas(j)
    r_ref[2, : plan.kept, :] = (dk_ref[...] * SCALE).astype(BF16)
    r_ref[3, : plan.kept, :] = dv_ref[...].astype(BF16)
    for at in range(4):
        r_ref[at, plan.kept :, :] = jnp.zeros((r_ref.shape[1] - plan.kept, DH), BF16)
    for slab in range(plan.slabs):
        spread(plan, slab, shard_counts[2 * slab], shard_counts[2 * slab + 1], r_ref, x_ref)

    for k in range(peers):
        first = pl.ds(plan.first_row(k), rows)
        for at in range(4):
            outs[k][at * rows : (at + 1) * rows, :] = x_ref[at, first, :]
    total = jnp.sum(sink_sum, axis=1, keepdims=True)
    row = lax.broadcasted_iota(jnp.int32, sink_out.shape, 0)
    sink_out[...] = jnp.where(row == local_head, total, 0.0)


def attention(plan, head, sink_logits, bufs, counts):
    out = jax.ShapeDtypeStruct((4 * plan.rows, DH), BF16)
    kept = plan.kept
    reach = kept - KEEP + 2 * plan.capacity + CUT
    sink_rows = -(-plan.group_heads // 8) * 8
    shapes = (out,) * plan.peers + (jax.ShapeDtypeStruct((sink_rows, DH), F32),)
    if head == 0:
        shapes += (jax.ShapeDtypeStruct((plan.peers * COUNT_ROWS, DH), BF16),)
    given = bufs if head == 0 else [*bufs, counts]
    results = pl.pallas_call(
        functools.partial(attention_kernel, plan, head),
        out_shape=shapes,
        in_specs=[pl.BlockSpec(memory_space=pltpu.SMEM)] + [IN_VMEM] * len(given),
        out_specs=(IN_VMEM,) * len(shapes),
        scratch_shapes=[
            pltpu.VMEM((4, plan.slots, DH), BF16),
            pltpu.VMEM((4, reach, DH), BF16),
            pltpu.VMEM((DH, kept), BF16),
            pltpu.VMEM((DH, kept), BF16),
            pltpu.VMEM((2, kept, QB), F32),
            pltpu.VMEM((kept, DH), F32),
            pltpu.VMEM((kept, DH), F32),
            pltpu.VMEM((4, reach, DH), BF16),
        ],
        compiler_params=pltpu.CompilerParams(vmem_limit_bytes=24 << 20),
    )(sink_logits, *given)
    blocks, sink_part = results[: plan.peers], results[plan.peers]
    return blocks, sink_part, results[-1] if head == 0 else counts


def unpack_kernel(plan, head, peers, carried, *refs):
    bufs = refs[: len(peers)]
    sem = refs[-1]
    outs = refs[len(peers) + (4 if carried else 0) : -1]
    rows = plan.rows
    copies = []
    for k, buf in zip(peers, bufs):
        for at, out in enumerate(outs):
            copies.append(
                pltpu.make_async_copy(
                    buf.at[pl.ds(at * rows, rows), :],
                    out.at[0, :, pl.ds(plan.column(k, head), DH)],
                    sem,
                )
            )
    run_copies(copies)


def unpack(plan, head, peers, bufs, held, features):
    out = jax.ShapeDtypeStruct((1, plan.rows, features), BF16)
    carried = held is not None
    held = held if carried else ()
    return pl.pallas_call(
        functools.partial(unpack_kernel, plan, head, peers, carried),
        out_shape=(out,) * 4,
        in_specs=[IN_VMEM] * len(peers) + [ANY] * len(held),
        out_specs=(ANY,) * 4,
        scratch_shapes=[pltpu.SemaphoreType.DMA(())],
        input_output_aliases={len(peers) + at: at for at in range(len(held))},
        compiler_params=pltpu.CompilerParams(vmem_limit_bytes=6 << 20),
    )(*(bufs[k] for k in peers), *held)


def exchange(plan, bufs, order):
    axes = ("seq", "tensor")
    swapped = dict(bufs)
    for k in order:
        pairs = [(i, i ^ k) for i in range(plan.peers)]
        swapped[k] = lax.ppermute(bufs[k], axes, pairs)
    return swapped


def swap_sum(value, axis, step):
    pairs = [(i, i ^ step) for i in range(lax.axis_size(axis))]
    return value + lax.ppermute(value, axis, pairs)


def steps_of(axis):
    size = lax.axis_size(axis)
    return [1 << bit for bit in reversed(range(size.bit_length() - 1))]


def by_heads(queries, key_vectors, values, out_grad, positions, sink_logits):
    seq, tensor = lax.axis_size("seq"), lax.axis_size("tensor")
    rows, features = queries.shape[1:]
    plan = Plan(seq, tensor, rows, features)
    arrays = (queries, key_vectors, values, out_grad)
    others = range(1, plan.peers)
    order = sorted(others, key=lambda k: (bin(k).count("1"), -k))
    first = tuple(k for k in (plan.peers // 2, 1, plan.peers // 2 + tensor) if k in order)
    rest = tuple(k for k in order if k not in first) + (0,)
    received = []
    for head in range(plan.heads):
        groups = (first, rest) if head == 0 else (first + rest,)
        blocks = {}
        for group in groups:
            packed = pack(plan, head, group, arrays, positions)
            blocks.update(zip(group, packed))
        received.append(exchange(plan, blocks, first + rest[:-1]))
    outs = None
    sink_sum = None
    counts = None
    for head in range(plan.heads):
        last = head == plan.heads - 1
        bufs = [received[head][k] for k in range(plan.peers)]
        results, sink_part, counts = attention(plan, head, sink_logits, bufs, counts)
        sink_sum = sink_part if sink_sum is None else sink_sum + sink_part
        if last:
            for axis in ("seq", "dp"):
                for step in steps_of(axis):
                    sink_sum = swap_sum(sink_sum, axis, step)
        results = exchange(plan, dict(enumerate(results)), order)
        if last:
            outs = unpack(plan, head, (0, *order[:-2]), results, outs, features)
            outs = unpack(plan, head, tuple(order[-2:]), results, outs, features)
        else:
            outs = unpack(plan, head, (0, *order), results, outs, features)
    return (*outs, sink_sum[: plan.group_heads, 0])


def block_scores(query_block, query_pos, key_block, key_pos):
    raw_scores = jnp.einsum(
        "ghd,khd->hgk", query_block, key_block, preferred_element_type=jnp.float32
    )
    scores = raw_scores * DH ** (-0.5)
    visible = (key_pos[None, :] <= query_pos[:, None]) & (key_pos[None, :] >= 0)
    return jnp.where(visible[None], scores, -1e30)


def row_stats(query_rows, query_pos, last_slab, key_all, key_pos, sink_logits, key_span):
    head_count = query_rows.shape[1]
    row_count = query_rows.shape[0]
    start_max = jnp.broadcast_to(sink_logits[:, None], (head_count, row_count))
    start_total = jnp.zeros((head_count, row_count), jnp.float32)

    def row_one_block(block, loop_state):
        row_max, row_total = loop_state
        key_block = lax.dynamic_slice_in_dim(key_all, block * key_span, key_span, 0)
        pos_block = lax.dynamic_slice_in_dim(key_pos, block * key_span, key_span, 0)
        scores = block_scores(query_rows, query_pos, key_block, pos_block)
        new_max = jnp.maximum(row_max, jnp.max(scores, axis=2))
        row_total = row_total * jnp.exp(row_max - new_max) + jnp.sum(
            jnp.exp(scores - new_max[:, :, None]), axis=2
        )
        return (new_max, row_total)

    row_max, row_total = lax.fori_loop(0, last_slab + 1, row_one_block, (start_max, start_total))
    return (row_max, row_total + jnp.exp(sink_logits[:, None] - row_max))


def attend_rows(
    query_rows, query_pos, last_slab, key_all, value_all, key_pos, row_max, row_total, key_span
):

    def attend_one_block(block, summed):
        key_block = lax.dynamic_slice_in_dim(key_all, block * key_span, key_span, 0)
        value_block = lax.dynamic_slice_in_dim(value_all, block * key_span, key_span, 0)
        pos_block = lax.dynamic_slice_in_dim(key_pos, block * key_span, key_span, 0)
        scores = block_scores(query_rows, query_pos, key_block, pos_block)
        weights_half = (jnp.exp(scores - row_max[:, :, None]) / row_total[:, :, None]).astype(
            jnp.bfloat16
        )
        return summed + jnp.einsum(
            "hgk,khd->ghd", weights_half, value_block, preferred_element_type=jnp.float32
        )

    summed = lax.fori_loop(
        0, last_slab + 1, attend_one_block, jnp.zeros(query_rows.shape, jnp.float32)
    )
    return summed.astype(jnp.bfloat16)


def query_grads(
    query_rows,
    grad_rows,
    query_pos,
    last_slab,
    key_all,
    value_all,
    key_pos,
    row_max,
    row_total,
    delta_rows,
    key_span,
    key_sums,
    value_sums,
):

    def query_one_block(block, loop_state):
        query_sum, key_state, value_state = loop_state
        key_block = lax.dynamic_slice_in_dim(key_all, block * key_span, key_span, 0)
        value_block = lax.dynamic_slice_in_dim(value_all, block * key_span, key_span, 0)
        pos_block = lax.dynamic_slice_in_dim(key_pos, block * key_span, key_span, 0)
        scores = block_scores(query_rows, query_pos, key_block, pos_block)
        weights_full = jnp.exp(scores - row_max[:, :, None]) / row_total[:, :, None]
        value_dots = jnp.einsum(
            "ghd,khd->hgk", grad_rows, value_block, preferred_element_type=jnp.float32
        )
        score_grad = (weights_full * (value_dots - delta_rows[:, :, None]) * DH ** (-0.5)).astype(
            jnp.bfloat16
        )
        query_sum = query_sum + jnp.einsum(
            "hgk,khd->ghd", score_grad, key_block, preferred_element_type=jnp.float32
        )
        return (query_sum, key_state, value_state)

    start = (jnp.zeros(query_rows.shape, jnp.float32), key_sums, value_sums)
    query_sum, key_sums, value_sums = lax.fori_loop(0, last_slab + 1, query_one_block, start)
    return (query_sum.astype(jnp.bfloat16), key_sums, value_sums)


def key_grads(
    key_rows,
    value_rows,
    key_pos,
    query_all,
    grad_all,
    query_pos_all,
    max_all,
    total_all,
    delta_all,
    first_slab,
    slab_count,
    query_span,
):

    def key_one_block(block, loop_state):
        key_sum, value_sum = loop_state
        query_block = lax.dynamic_slice_in_dim(query_all, block * query_span, query_span, 0)
        grad_block = lax.dynamic_slice_in_dim(grad_all, block * query_span, query_span, 0)
        pos_block = lax.dynamic_slice_in_dim(query_pos_all, block * query_span, query_span, 0)
        max_block = lax.dynamic_slice_in_dim(max_all, block * query_span, query_span, 1)
        total_block = lax.dynamic_slice_in_dim(total_all, block * query_span, query_span, 1)
        delta_block = lax.dynamic_slice_in_dim(delta_all, block * query_span, query_span, 1)
        scores = block_scores(query_block, pos_block, key_rows, key_pos)
        weights_full = jnp.exp(scores - max_block[:, :, None]) / total_block[:, :, None]
        value_dots = jnp.einsum(
            "ghd,khd->hgk", grad_block, value_rows, preferred_element_type=jnp.float32
        )
        score_grad = (weights_full * (value_dots - delta_block[:, :, None]) * DH ** (-0.5)).astype(
            jnp.bfloat16
        )
        key_sum = key_sum + jnp.einsum(
            "hgk,ghd->khd", score_grad, query_block, preferred_element_type=jnp.float32
        )
        value_sum = value_sum + jnp.einsum(
            "hgk,ghd->khd",
            weights_full.astype(jnp.bfloat16),
            grad_block,
            preferred_element_type=jnp.float32,
        )
        return (key_sum, value_sum)

    zeros = jnp.zeros(key_rows.shape, jnp.float32)
    return lax.fori_loop(first_slab, slab_count, key_one_block, (zeros, zeros))


def by_rows(queries, key_vectors, values, out_grad, positions, sink_logits):
    queries, key_vectors, values, out_grad = (
        lax.all_to_all(queries, "tensor", split_axis=2, concat_axis=1, tiled=True),
        lax.all_to_all(key_vectors, "tensor", split_axis=2, concat_axis=1, tiled=True),
        lax.all_to_all(values, "tensor", split_axis=2, concat_axis=1, tiled=True),
        lax.all_to_all(out_grad, "tensor", split_axis=2, concat_axis=1, tiled=True),
    )
    capacity = queries.shape[1]
    features = queries.shape[2]
    head_count = features // DH
    key_span = 2 * capacity
    seq_count = lax.axis_size("seq")
    seq_index = lax.axis_index("seq")
    query_rows = queries[0].reshape(capacity, head_count, DH)
    key_rows = key_vectors[0].reshape(capacity, head_count, DH)
    value_rows = values[0].reshape(capacity, head_count, DH)
    grad_rows = out_grad[0].reshape(capacity, head_count, DH)
    pos_rows = positions[0]
    key_all, value_all, key_pos = (
        lax.all_gather(key_rows, "seq", axis=0, tiled=True),
        lax.all_gather(value_rows, "seq", axis=0, tiled=True),
        lax.all_gather(pos_rows, "seq", axis=0, tiled=True),
    )
    own_slab = seq_index // 2
    groups = (query_rows, grad_rows, pos_rows, own_slab)
    key_sums = None
    value_sums = None
    sink_sum = jnp.zeros((head_count,), jnp.float32)
    group_rows, group_grads, group_pos, last_slab = groups
    row_max, row_total = row_stats(
        group_rows, group_pos, last_slab, key_all, key_pos, sink_logits, key_span
    )
    attended = attend_rows(
        group_rows, group_pos, last_slab, key_all, value_all, key_pos, row_max, row_total, key_span
    )
    delta_rows = jnp.sum(attended.astype(jnp.float32) * group_grads.astype(jnp.float32), axis=2).T
    sink_sum = sink_sum - jnp.sum(
        jnp.exp(sink_logits[:, None] - row_max) / row_total * delta_rows, axis=1
    )
    query_grad, key_sums, value_sums = query_grads(
        group_rows,
        group_grads,
        group_pos,
        last_slab,
        key_all,
        value_all,
        key_pos,
        row_max,
        row_total,
        delta_rows,
        key_span,
        key_sums,
        value_sums,
    )
    results = (attended, query_grad, row_max, row_total, delta_rows)
    attended = results[0]
    query_grad = results[1]
    own_max = results[2]
    own_total = results[3]
    own_delta = results[4]
    query_all, grad_all, query_pos_all = (
        lax.all_gather(query_rows, "seq", axis=0, tiled=True),
        lax.all_gather(grad_rows, "seq", axis=0, tiled=True),
        lax.all_gather(pos_rows, "seq", axis=0, tiled=True),
    )
    max_all, total_all, delta_all = (
        lax.all_gather(own_max, "seq", axis=1, tiled=True),
        lax.all_gather(own_total, "seq", axis=1, tiled=True),
        lax.all_gather(own_delta, "seq", axis=1, tiled=True),
    )
    key_sum, value_sum = key_grads(
        key_rows,
        value_rows,
        pos_rows,
        query_all,
        grad_all,
        query_pos_all,
        max_all,
        total_all,
        delta_all,
        own_slab,
        seq_count // 2,
        key_span,
    )
    key_grad, value_grad = (
        lax.all_to_all(
            key_sum.astype(jnp.bfloat16).reshape(1, capacity, features),
            "tensor",
            split_axis=1,
            concat_axis=2,
            tiled=True,
        ),
        lax.all_to_all(
            value_sum.astype(jnp.bfloat16).reshape(1, capacity, features),
            "tensor",
            split_axis=1,
            concat_axis=2,
            tiled=True,
        ),
    )
    attended, query_grad = (
        lax.all_to_all(
            attended.reshape(1, capacity, features),
            "tensor",
            split_axis=1,
            concat_axis=2,
            tiled=True,
        ),
        lax.all_to_all(
            query_grad.reshape(1, capacity, features),
            "tensor",
            split_axis=1,
            concat_axis=2,
            tiled=True,
        ),
    )
    sink_grad = lax.psum(sink_sum, ("seq", "dp"))
    return (attended, query_grad, key_grad, value_grad, sink_grad)


def solution(mesh):
    placed = (
        P("dp", ("seq", "tensor"), None),
        P("dp", ("seq", "tensor"), None),
        P("dp", ("seq", "tensor"), None),
        P("dp", ("seq", "tensor"), None),
        P("dp", "seq"),
        P("tensor"),
    )
    sizes = (mesh.shape["seq"], mesh.shape["tensor"], mesh.shape["dp"])

    def on_device(queries, *rest):
        heads = queries.shape[2] // DH
        even = all(size & (size - 1) == 0 for size in sizes)
        rows = queries.shape[1]
        capacity = rows * sizes[1]
        aligned = rows % 16 == 0 and rows <= 256 and capacity % CUT == 0
        aligned = aligned and sizes[0] > 1 and capacity < KEEP <= 4 * capacity // 3
        if even and aligned and heads % (sizes[0] * sizes[1]) == 0:
            return by_heads(queries, *rest)
        return by_rows(queries, *rest)

    return jax.shard_map(
        on_device,
        mesh=mesh,
        in_specs=placed,
        out_specs=(
            P("dp", ("seq", "tensor"), None),
            P("dp", ("seq", "tensor"), None),
            P("dp", ("seq", "tensor"), None),
            P("dp", ("seq", "tensor"), None),
            P("tensor"),
        ),
        check_vma=False,
    )
```

```python
import functools

import jax
import jax.numpy as jnp
from jax import lax
from jax.experimental import pallas as pl
from jax.experimental.pallas import tpu as pltpu
from jax.sharding import PartitionSpec as P


DH = 128
SCALE = DH ** (-0.5)
NEG = -1e30
LOG2E = 1.4426950408889634
KEEP = 512
QB = 256
CUT = 128
COUNT_ROWS = 8
F32 = jnp.float32
BF16 = jnp.bfloat16
ANY = pl.BlockSpec(memory_space=pl.ANY)
IN_HBM = pl.BlockSpec(memory_space=pltpu.HBM)
IN_VMEM = pl.BlockSpec(memory_space=pltpu.VMEM)
NT = (((1,), (1,)), ((), ()))
NN = (((1,), (0,)), ((), ()))


def dot(a, b, dims):
    return lax.dot_general(a, b, dims, preferred_element_type=F32)


class Plan:
    def __init__(self, seq, tensor, rows, features):
        self.seq, self.tensor, self.rows = seq, tensor, rows
        self.peers = seq * tensor
        self.slots = rows * self.peers
        self.capacity = rows * tensor
        self.slabs = seq // 2
        self.kept = self.slabs * KEEP
        self.group_heads = features // DH // tensor
        self.heads = self.group_heads // seq

    def where(self):
        return lax.axis_index("seq"), lax.axis_index("tensor")

    def peer(self, k):
        seq_index, tensor_index = self.where()
        return seq_index ^ (k // self.tensor), tensor_index ^ (k % self.tensor)

    def column(self, k, head):
        seq_index, tensor_index = self.peer(k)
        owned = tensor_index * self.group_heads + seq_index * self.heads + head
        return pl.multiple_of(owned * DH, DH)

    def first_row(self, k):
        seq_index, tensor_index = self.peer(k)
        return pl.multiple_of((seq_index * self.tensor + tensor_index) * self.rows, 16)

    def first_count(self, k):
        seq_index, tensor_index = self.peer(k)
        return pl.multiple_of((seq_index * self.tensor + tensor_index) * COUNT_ROWS, 8)


def run_copies(copies):
    for copy in copies:
        copy.start()
    for copy in copies:
        copy.wait()


def pack_kernel(plan, head, peers, *refs):
    arrays, positions_hbm = refs[:4], refs[4]
    outs, positions, sem, positions_sem = refs[5:-3], refs[-3], refs[-2], refs[-1]
    rows = plan.rows
    copies = []
    for k, out in zip(peers, outs):
        for at, array in enumerate(arrays):
            copies.append(
                pltpu.make_async_copy(
                    array.at[0, :, pl.ds(plan.column(k, head), DH)],
                    out.at[pl.ds(at * rows, rows), :],
                    sem,
                )
            )
    if head > 0:
        run_copies(copies)
        return
    fetch = pltpu.make_async_copy(positions_hbm, positions, positions_sem)
    fetch.start()
    for copy in copies:
        copy.start()
    _, tensor_index = plan.where()
    slot = lax.broadcasted_iota(jnp.int32, positions.shape, 1) - tensor_index * rows
    fetch.wait()
    filled = (positions[...] >= 0) & (slot >= 0) & (slot < rows)
    count = jnp.sum(filled.astype(F32), axis=1, keepdims=True)
    tile = jnp.broadcast_to(count, (COUNT_ROWS, DH)).astype(BF16)
    for out in outs:
        out[4 * rows :, :] = tile
    for copy in copies:
        copy.wait()


def pack(plan, head, peers, arrays, positions):
    out = jax.ShapeDtypeStruct((4 * plan.rows + (COUNT_ROWS if head == 0 else 0), DH), BF16)
    return pl.pallas_call(
        functools.partial(pack_kernel, plan, head, peers),
        out_shape=(out,) * len(peers),
        in_specs=[IN_HBM] * 5,
        out_specs=(IN_VMEM,) * len(peers),
        scratch_shapes=[
            pltpu.VMEM(positions.shape, jnp.int32),
            pltpu.SemaphoreType.DMA(()),
            pltpu.SemaphoreType.DMA(()),
        ],
        compiler_params=pltpu.CompilerParams(vmem_limit_bytes=6 << 20),
    )(*(pltpu.with_memory_space_constraint(value, pltpu.HBM) for value in (*arrays, positions)))


def selection(rows, columns, shift, limit=None):
    i = lax.broadcasted_iota(jnp.int32, (rows, columns), 0)
    j = lax.broadcasted_iota(jnp.int32, (rows, columns), 1)
    chosen = j == i + shift
    if limit is not None:
        chosen = chosen & (i < limit)
    return jnp.where(chosen, 1.0, 0.0).astype(BF16)


def compact(plan, slab, first_count, x_ref, y_ref):
    capacity = plan.capacity
    base = slab * KEEP
    here = slab * 2 * capacity
    aligned = pl.multiple_of((first_count // 16) * 16, 16)
    rest = first_count - aligned
    head_part = selection(CUT, CUT, -rest)
    cross_part = selection(CUT, 2 * CUT, CUT - rest)
    row = lax.broadcasted_iota(jnp.int32, (CUT, DH), 0)
    for at in range(4):
        y_ref[at, base : base + capacity, :] = x_ref[at, here : here + capacity, :]
        for part in range(capacity // CUT):
            second = here + capacity + part * CUT
            target = pl.ds(pl.multiple_of(base + aligned + part * CUT, 16), CUT)
            if part == 0:
                moved = dot(head_part, x_ref[at, second : second + CUT, :], NN)
                old = y_ref[at, target, :].astype(F32)
                moved = jnp.where(row < rest, old, moved)
            else:
                moved = dot(cross_part, x_ref[at, second - CUT : second + CUT, :], NN)
            y_ref[at, target, :] = moved.astype(BF16)


def spread(plan, slab, first_count, second_count, r_ref, x_ref):
    capacity = plan.capacity
    base = slab * KEEP
    here = slab * 2 * capacity
    aligned = pl.multiple_of((first_count // 16) * 16, 16)
    rest = first_count - aligned
    row = lax.broadcasted_iota(jnp.int32, (capacity, DH), 0)
    for at in range(4):
        kept = r_ref[at, base : base + capacity, :]
        kept = jnp.where(row < first_count, kept.astype(F32), 0.0).astype(BF16)
        x_ref[at, here : here + capacity, :] = kept
    for part in range(capacity // CUT):
        chosen = selection(CUT, 2 * CUT, rest, second_count - part * CUT)
        source = pl.ds(pl.multiple_of(base + aligned + part * CUT, 16), 2 * CUT)
        target = here + capacity + part * CUT
        for at in range(4):
            moved = dot(chosen, r_ref[at, source, :], NN)
            x_ref[at, target : target + CUT, :] = moved.astype(BF16)


def attention_kernel(plan, head, *refs):
    peers, rows = plan.peers, plan.rows
    sink_ref, bufs, refs = refs[0], refs[1 : 1 + peers], refs[1 + peers :]
    if head > 0:
        count_ref, *refs = refs
    outs, sink_out, refs = refs[:peers], refs[peers], refs[peers + 1 :]
    if head == 0:
        count_ref, *refs = refs
        for k in range(peers):
            first = pl.ds(plan.first_count(k), COUNT_ROWS)
            count_ref[first, :] = bufs[k][4 * rows :, :]
    x_ref, y_ref, kt_ref, vt_ref, s_ref, dk_ref, dv_ref, r_ref = refs
    for k in range(peers):
        first = pl.ds(plan.first_row(k), rows)
        for at in range(4):
            x_ref[at, first, :] = bufs[k][at * rows : (at + 1) * rows, :]

    shard_counts = []
    for shard in range(plan.seq):
        first = shard * plan.tensor * COUNT_ROWS
        tiles = count_ref[first : first + plan.tensor * COUNT_ROWS, :].astype(F32)
        shard_counts.append((jnp.sum(tiles) * (1.0 / (COUNT_ROWS * DH))).astype(jnp.int32))
    for slab in range(plan.slabs):
        compact(plan, slab, shard_counts[2 * slab], x_ref, y_ref)

    own_seq, _ = plan.where()
    local_head = own_seq * plan.heads + head
    sink = sink_ref[local_head]
    kt_ref[...] = y_ref[1, : plan.kept, :].T
    vt_ref[...] = y_ref[2, : plan.kept, :].T
    behind = lax.broadcasted_iota(jnp.int32, (QB, QB), 0) > lax.broadcasted_iota(
        jnp.int32, (QB, QB), 1
    )
    blocks = plan.kept // QB
    sink_sum = jnp.zeros((1, QB), F32)
    state = {}

    def at_block(b):
        return slice(b * QB, (b + 1) * QB)

    def held(j, b):
        return (j % 2, at_block(b))

    def start(j):
        state[j] = dict(
            q=y_ref[0, at_block(j), :],
            g=y_ref[3, at_block(j), :],
            top=None,
            total=None,
            attended=None,
            query_grad=None,
        )

    def add(now, more):
        return more if now is None else now + more

    def scores(j, b):
        own = state[j]
        s = dot(y_ref[1, at_block(b), :], own["q"], NT)
        if b == j:
            s = jnp.where(behind, NEG, s)
        s_ref[held(j, b)] = s
        top = jnp.max(s.reshape(QB // 8, 8, QB), axis=0)
        own["top"] = top if own["top"] is None else jnp.maximum(own["top"], top)

    def row_max(j):
        own = state[j]
        top = jnp.max(own["top"], axis=0, keepdims=True) * (SCALE * LOG2E)
        own["max"] = jnp.maximum(top, sink * LOG2E)

    def exponentials(j, b):
        own = state[j]
        e = jnp.exp2(s_ref[held(j, b)] * (SCALE * LOG2E) - own["max"])
        s_ref[held(j, b)] = e
        own["total"] = add(own["total"], jnp.sum(e.reshape(QB // 8, 8, QB), axis=0))

    def row_total(j):
        own = state[j]
        own["sink"] = jnp.exp2(sink * LOG2E - own["max"])
        own["inverse"] = 1.0 / (jnp.sum(own["total"], axis=0, keepdims=True) + own["sink"])

    def weigh(j, b):
        own = state[j]
        w = s_ref[held(j, b)] * own["inverse"]
        s_ref[held(j, b)] = w
        half = w.astype(BF16)
        own["attended"] = add(own["attended"], dot(vt_ref[:, at_block(b)], half, NN))
        dv = dot(half, own["g"], NN)
        dv_ref[at_block(b), :] = dv if b == j else dv_ref[at_block(b), :] + dv

    def deltas(j):
        own = state[j]
        attended = own["attended"].astype(BF16)
        r_ref[0, at_block(j), :] = attended.T
        own["delta"] = jnp.sum(
            attended.astype(F32) * own["g"].astype(F32).T, axis=0, keepdims=True
        )
        return own["sink"] * own["inverse"] * own["delta"]

    def gradients(j, b):
        own = state[j]
        dp = dot(y_ref[2, at_block(b), :], own["g"], NT)
        ds = (s_ref[held(j, b)] * (dp - own["delta"])).astype(BF16)
        own["query_grad"] = add(own["query_grad"], dot(kt_ref[:, at_block(b)], ds, NN))
        dk = dot(ds, own["q"], NN)
        dk_ref[at_block(b), :] = dk if b == j else dk_ref[at_block(b), :] + dk

    def finish(j):
        r_ref[1, at_block(j), :] = (state[j]["query_grad"] * SCALE).astype(BF16).T

    for j in range(blocks + 1):
        if j < blocks:
            start(j)
            for b in range(j + 1):
                scores(j, b)
            row_max(j)
        for b in range(j + 1):
            if j < blocks:
                exponentials(j, b)
            if b < j:
                gradients(j - 1, b)
        if j > 0:
            finish(j - 1)
        if j < blocks:
            row_total(j)
            for b in range(j + 1):
                weigh(j, b)
            sink_sum = sink_sum - deltas(j)
    r_ref[2, : plan.kept, :] = (dk_ref[...] * SCALE).astype(BF16)
    r_ref[3, : plan.kept, :] = dv_ref[...].astype(BF16)
    for at in range(4):
        r_ref[at, plan.kept :, :] = jnp.zeros((r_ref.shape[1] - plan.kept, DH), BF16)
    for slab in range(plan.slabs):
        spread(plan, slab, shard_counts[2 * slab], shard_counts[2 * slab + 1], r_ref, x_ref)

    for k in range(peers):
        first = pl.ds(plan.first_row(k), rows)
        for at in range(4):
            outs[k][at * rows : (at + 1) * rows, :] = x_ref[at, first, :]
    total = jnp.sum(sink_sum, axis=1, keepdims=True)
    row = lax.broadcasted_iota(jnp.int32, sink_out.shape, 0)
    sink_out[...] = jnp.where(row == local_head, total, 0.0)


def attention(plan, head, sink_logits, bufs, counts):
    out = jax.ShapeDtypeStruct((4 * plan.rows, DH), BF16)
    kept = plan.kept
    reach = kept - KEEP + 2 * plan.capacity + CUT
    sink_rows = -(-plan.group_heads // 8) * 8
    shapes = (out,) * plan.peers + (jax.ShapeDtypeStruct((sink_rows, DH), F32),)
    if head == 0:
        shapes += (jax.ShapeDtypeStruct((plan.peers * COUNT_ROWS, DH), BF16),)
    given = bufs if head == 0 else [*bufs, counts]
    results = pl.pallas_call(
        functools.partial(attention_kernel, plan, head),
        out_shape=shapes,
        in_specs=[pl.BlockSpec(memory_space=pltpu.SMEM)] + [IN_VMEM] * len(given),
        out_specs=(IN_VMEM,) * len(shapes),
        scratch_shapes=[
            pltpu.VMEM((4, plan.slots, DH), BF16),
            pltpu.VMEM((4, reach, DH), BF16),
            pltpu.VMEM((DH, kept), BF16),
            pltpu.VMEM((DH, kept), BF16),
            pltpu.VMEM((2, kept, QB), F32),
            pltpu.VMEM((kept, DH), F32),
            pltpu.VMEM((kept, DH), F32),
            pltpu.VMEM((4, reach, DH), BF16),
        ],
        compiler_params=pltpu.CompilerParams(vmem_limit_bytes=24 << 20),
    )(sink_logits, *given)
    blocks, sink_part = results[: plan.peers], results[plan.peers]
    return blocks, sink_part, results[-1] if head == 0 else counts


def unpack_kernel(plan, head, peers, carried, *refs):
    bufs = refs[: len(peers)]
    sem = refs[-1]
    outs = refs[len(peers) + (4 if carried else 0) : -1]
    rows = plan.rows
    copies = []
    for k, buf in zip(peers, bufs):
        for at, out in enumerate(outs):
            copies.append(
                pltpu.make_async_copy(
                    buf.at[pl.ds(at * rows, rows), :],
                    out.at[0, :, pl.ds(plan.column(k, head), DH)],
                    sem,
                )
            )
    run_copies(copies)


def unpack(plan, head, peers, bufs, held, features):
    out = jax.ShapeDtypeStruct((1, plan.rows, features), BF16)
    carried = held is not None
    held = held if carried else ()
    return pl.pallas_call(
        functools.partial(unpack_kernel, plan, head, peers, carried),
        out_shape=(out,) * 4,
        in_specs=[IN_VMEM] * len(peers) + [ANY] * len(held),
        out_specs=(ANY,) * 4,
        scratch_shapes=[pltpu.SemaphoreType.DMA(())],
        input_output_aliases={len(peers) + at: at for at in range(len(held))},
        compiler_params=pltpu.CompilerParams(vmem_limit_bytes=6 << 20),
    )(*(bufs[k] for k in peers), *held)


def exchange(plan, bufs, order):
    axes = ("seq", "tensor")
    swapped = dict(bufs)
    for k in order:
        pairs = [(i, i ^ k) for i in range(plan.peers)]
        swapped[k] = lax.ppermute(bufs[k], axes, pairs)
    return swapped


def swap_sum(value, axis, step):
    pairs = [(i, i ^ step) for i in range(lax.axis_size(axis))]
    return value + lax.ppermute(value, axis, pairs)


def steps_of(axis):
    size = lax.axis_size(axis)
    return [1 << bit for bit in reversed(range(size.bit_length() - 1))]


def by_heads(queries, key_vectors, values, out_grad, positions, sink_logits):
    seq, tensor = lax.axis_size("seq"), lax.axis_size("tensor")
    rows, features = queries.shape[1:]
    plan = Plan(seq, tensor, rows, features)
    arrays = (queries, key_vectors, values, out_grad)
    others = range(1, plan.peers)
    order = sorted(others, key=lambda k: (bin(k).count("1"), -k))
    first = tuple(k for k in (plan.peers // 2, 1, plan.peers // 2 + tensor) if k in order)
    rest = tuple(k for k in order if k not in first) + (0,)
    received = []
    for head in range(plan.heads):
        groups = (first, rest) if head == 0 else (first + rest,)
        blocks = {}
        for group in groups:
            packed = pack(plan, head, group, arrays, positions)
            blocks.update(zip(group, packed))
        received.append(exchange(plan, blocks, first + rest[:-1]))
    outs = None
    sink_sum = None
    counts = None
    for head in range(plan.heads):
        last = head == plan.heads - 1
        bufs = [received[head][k] for k in range(plan.peers)]
        results, sink_part, counts = attention(plan, head, sink_logits, bufs, counts)
        sink_sum = sink_part if sink_sum is None else sink_sum + sink_part
        if last:
            for axis in ("seq", "dp"):
                for step in steps_of(axis):
                    sink_sum = swap_sum(sink_sum, axis, step)
        results = exchange(plan, dict(enumerate(results)), order)
        if last:
            outs = unpack(plan, head, (0, *order[:-1]), results, outs, features)
            outs = unpack(plan, head, tuple(order[-1:]), results, outs, features)
        else:
            outs = unpack(plan, head, (0, *order), results, outs, features)
    return (*outs, sink_sum[: plan.group_heads, 0])


def block_scores(query_block, query_pos, key_block, key_pos):
    raw_scores = jnp.einsum(
        "ghd,khd->hgk", query_block, key_block, preferred_element_type=jnp.float32
    )
    scores = raw_scores * DH ** (-0.5)
    visible = (key_pos[None, :] <= query_pos[:, None]) & (key_pos[None, :] >= 0)
    return jnp.where(visible[None], scores, -1e30)


def row_stats(query_rows, query_pos, last_slab, key_all, key_pos, sink_logits, key_span):
    head_count = query_rows.shape[1]
    row_count = query_rows.shape[0]
    start_max = jnp.broadcast_to(sink_logits[:, None], (head_count, row_count))
    start_total = jnp.zeros((head_count, row_count), jnp.float32)

    def row_one_block(block, loop_state):
        row_max, row_total = loop_state
        key_block = lax.dynamic_slice_in_dim(key_all, block * key_span, key_span, 0)
        pos_block = lax.dynamic_slice_in_dim(key_pos, block * key_span, key_span, 0)
        scores = block_scores(query_rows, query_pos, key_block, pos_block)
        new_max = jnp.maximum(row_max, jnp.max(scores, axis=2))
        row_total = row_total * jnp.exp(row_max - new_max) + jnp.sum(
            jnp.exp(scores - new_max[:, :, None]), axis=2
        )
        return (new_max, row_total)

    row_max, row_total = lax.fori_loop(0, last_slab + 1, row_one_block, (start_max, start_total))
    return (row_max, row_total + jnp.exp(sink_logits[:, None] - row_max))


def attend_rows(
    query_rows, query_pos, last_slab, key_all, value_all, key_pos, row_max, row_total, key_span
):

    def attend_one_block(block, summed):
        key_block = lax.dynamic_slice_in_dim(key_all, block * key_span, key_span, 0)
        value_block = lax.dynamic_slice_in_dim(value_all, block * key_span, key_span, 0)
        pos_block = lax.dynamic_slice_in_dim(key_pos, block * key_span, key_span, 0)
        scores = block_scores(query_rows, query_pos, key_block, pos_block)
        weights_half = (jnp.exp(scores - row_max[:, :, None]) / row_total[:, :, None]).astype(
            jnp.bfloat16
        )
        return summed + jnp.einsum(
            "hgk,khd->ghd", weights_half, value_block, preferred_element_type=jnp.float32
        )

    summed = lax.fori_loop(
        0, last_slab + 1, attend_one_block, jnp.zeros(query_rows.shape, jnp.float32)
    )
    return summed.astype(jnp.bfloat16)


def query_grads(
    query_rows,
    grad_rows,
    query_pos,
    last_slab,
    key_all,
    value_all,
    key_pos,
    row_max,
    row_total,
    delta_rows,
    key_span,
    key_sums,
    value_sums,
):

    def query_one_block(block, loop_state):
        query_sum, key_state, value_state = loop_state
        key_block = lax.dynamic_slice_in_dim(key_all, block * key_span, key_span, 0)
        value_block = lax.dynamic_slice_in_dim(value_all, block * key_span, key_span, 0)
        pos_block = lax.dynamic_slice_in_dim(key_pos, block * key_span, key_span, 0)
        scores = block_scores(query_rows, query_pos, key_block, pos_block)
        weights_full = jnp.exp(scores - row_max[:, :, None]) / row_total[:, :, None]
        value_dots = jnp.einsum(
            "ghd,khd->hgk", grad_rows, value_block, preferred_element_type=jnp.float32
        )
        score_grad = (weights_full * (value_dots - delta_rows[:, :, None]) * DH ** (-0.5)).astype(
            jnp.bfloat16
        )
        query_sum = query_sum + jnp.einsum(
            "hgk,khd->ghd", score_grad, key_block, preferred_element_type=jnp.float32
        )
        return (query_sum, key_state, value_state)

    start = (jnp.zeros(query_rows.shape, jnp.float32), key_sums, value_sums)
    query_sum, key_sums, value_sums = lax.fori_loop(0, last_slab + 1, query_one_block, start)
    return (query_sum.astype(jnp.bfloat16), key_sums, value_sums)


def key_grads(
    key_rows,
    value_rows,
    key_pos,
    query_all,
    grad_all,
    query_pos_all,
    max_all,
    total_all,
    delta_all,
    first_slab,
    slab_count,
    query_span,
):

    def key_one_block(block, loop_state):
        key_sum, value_sum = loop_state
        query_block = lax.dynamic_slice_in_dim(query_all, block * query_span, query_span, 0)
        grad_block = lax.dynamic_slice_in_dim(grad_all, block * query_span, query_span, 0)
        pos_block = lax.dynamic_slice_in_dim(query_pos_all, block * query_span, query_span, 0)
        max_block = lax.dynamic_slice_in_dim(max_all, block * query_span, query_span, 1)
        total_block = lax.dynamic_slice_in_dim(total_all, block * query_span, query_span, 1)
        delta_block = lax.dynamic_slice_in_dim(delta_all, block * query_span, query_span, 1)
        scores = block_scores(query_block, pos_block, key_rows, key_pos)
        weights_full = jnp.exp(scores - max_block[:, :, None]) / total_block[:, :, None]
        value_dots = jnp.einsum(
            "ghd,khd->hgk", grad_block, value_rows, preferred_element_type=jnp.float32
        )
        score_grad = (weights_full * (value_dots - delta_block[:, :, None]) * DH ** (-0.5)).astype(
            jnp.bfloat16
        )
        key_sum = key_sum + jnp.einsum(
            "hgk,ghd->khd", score_grad, query_block, preferred_element_type=jnp.float32
        )
        value_sum = value_sum + jnp.einsum(
            "hgk,ghd->khd",
            weights_full.astype(jnp.bfloat16),
            grad_block,
            preferred_element_type=jnp.float32,
        )
        return (key_sum, value_sum)

    zeros = jnp.zeros(key_rows.shape, jnp.float32)
    return lax.fori_loop(first_slab, slab_count, key_one_block, (zeros, zeros))


def by_rows(queries, key_vectors, values, out_grad, positions, sink_logits):
    queries, key_vectors, values, out_grad = (
        lax.all_to_all(queries, "tensor", split_axis=2, concat_axis=1, tiled=True),
        lax.all_to_all(key_vectors, "tensor", split_axis=2, concat_axis=1, tiled=True),
        lax.all_to_all(values, "tensor", split_axis=2, concat_axis=1, tiled=True),
        lax.all_to_all(out_grad, "tensor", split_axis=2, concat_axis=1, tiled=True),
    )
    capacity = queries.shape[1]
    features = queries.shape[2]
    head_count = features // DH
    key_span = 2 * capacity
    seq_count = lax.axis_size("seq")
    seq_index = lax.axis_index("seq")
    query_rows = queries[0].reshape(capacity, head_count, DH)
    key_rows = key_vectors[0].reshape(capacity, head_count, DH)
    value_rows = values[0].reshape(capacity, head_count, DH)
    grad_rows = out_grad[0].reshape(capacity, head_count, DH)
    pos_rows = positions[0]
    key_all, value_all, key_pos = (
        lax.all_gather(key_rows, "seq", axis=0, tiled=True),
        lax.all_gather(value_rows, "seq", axis=0, tiled=True),
        lax.all_gather(pos_rows, "seq", axis=0, tiled=True),
    )
    own_slab = seq_index // 2
    groups = (query_rows, grad_rows, pos_rows, own_slab)
    key_sums = None
    value_sums = None
    sink_sum = jnp.zeros((head_count,), jnp.float32)
    group_rows, group_grads, group_pos, last_slab = groups
    row_max, row_total = row_stats(
        group_rows, group_pos, last_slab, key_all, key_pos, sink_logits, key_span
    )
    attended = attend_rows(
        group_rows, group_pos, last_slab, key_all, value_all, key_pos, row_max, row_total, key_span
    )
    delta_rows = jnp.sum(attended.astype(jnp.float32) * group_grads.astype(jnp.float32), axis=2).T
    sink_sum = sink_sum - jnp.sum(
        jnp.exp(sink_logits[:, None] - row_max) / row_total * delta_rows, axis=1
    )
    query_grad, key_sums, value_sums = query_grads(
        group_rows,
        group_grads,
        group_pos,
        last_slab,
        key_all,
        value_all,
        key_pos,
        row_max,
        row_total,
        delta_rows,
        key_span,
        key_sums,
        value_sums,
    )
    results = (attended, query_grad, row_max, row_total, delta_rows)
    attended = results[0]
    query_grad = results[1]
    own_max = results[2]
    own_total = results[3]
    own_delta = results[4]
    query_all, grad_all, query_pos_all = (
        lax.all_gather(query_rows, "seq", axis=0, tiled=True),
        lax.all_gather(grad_rows, "seq", axis=0, tiled=True),
        lax.all_gather(pos_rows, "seq", axis=0, tiled=True),
    )
    max_all, total_all, delta_all = (
        lax.all_gather(own_max, "seq", axis=1, tiled=True),
        lax.all_gather(own_total, "seq", axis=1, tiled=True),
        lax.all_gather(own_delta, "seq", axis=1, tiled=True),
    )
    key_sum, value_sum = key_grads(
        key_rows,
        value_rows,
        pos_rows,
        query_all,
        grad_all,
        query_pos_all,
        max_all,
        total_all,
        delta_all,
        own_slab,
        seq_count // 2,
        key_span,
    )
    key_grad, value_grad = (
        lax.all_to_all(
            key_sum.astype(jnp.bfloat16).reshape(1, capacity, features),
            "tensor",
            split_axis=1,
            concat_axis=2,
            tiled=True,
        ),
        lax.all_to_all(
            value_sum.astype(jnp.bfloat16).reshape(1, capacity, features),
            "tensor",
            split_axis=1,
            concat_axis=2,
            tiled=True,
        ),
    )
    attended, query_grad = (
        lax.all_to_all(
            attended.reshape(1, capacity, features),
            "tensor",
            split_axis=1,
            concat_axis=2,
            tiled=True,
        ),
        lax.all_to_all(
            query_grad.reshape(1, capacity, features),
            "tensor",
            split_axis=1,
            concat_axis=2,
            tiled=True,
        ),
    )
    sink_grad = lax.psum(sink_sum, ("seq", "dp"))
    return (attended, query_grad, key_grad, value_grad, sink_grad)


def solution(mesh):
    placed = (
        P("dp", ("seq", "tensor"), None),
        P("dp", ("seq", "tensor"), None),
        P("dp", ("seq", "tensor"), None),
        P("dp", ("seq", "tensor"), None),
        P("dp", "seq"),
        P("tensor"),
    )
    sizes = (mesh.shape["seq"], mesh.shape["tensor"], mesh.shape["dp"])

    def on_device(queries, *rest):
        heads = queries.shape[2] // DH
        even = all(size & (size - 1) == 0 for size in sizes)
        rows = queries.shape[1]
        capacity = rows * sizes[1]
        aligned = rows % 16 == 0 and rows <= 256 and capacity % CUT == 0
        aligned = aligned and sizes[0] > 1 and capacity < KEEP <= 4 * capacity // 3
        if even and aligned and heads % (sizes[0] * sizes[1]) == 0:
            return by_heads(queries, *rest)
        return by_rows(queries, *rest)

    return jax.shard_map(
        on_device,
        mesh=mesh,
        in_specs=placed,
        out_specs=(
            P("dp", ("seq", "tensor"), None),
            P("dp", ("seq", "tensor"), None),
            P("dp", ("seq", "tensor"), None),
            P("dp", ("seq", "tensor"), None),
            P("tensor"),
        ),
        check_vma=False,
    )
```
